128 devices in a mesh: row: 16 (over z_hi, y, core), col: 8 (over z_lo, x).
Axes of the slice: x: 4, y: 4, z: 4 (z_hi: 2, z_lo: 2; z = z_hi * 2 + z_lo), core: 2. Of those that a mesh axis runs over, the one named last changes fastest.
Arguments:
- tokens: bfloat16 [4096, 2048], P('row', 'col'), may hold values from -6 to 6
- attn_gain: float32 [2048], replicated, may hold values from 0.5 to 6, as said below
- mlp_gain: float32 [2048], replicated, may hold values from 0.5 to 1.5
- trainer_qkv: float32 [2048, 3072], P(('row', 'col')), may hold values from -0.125 to 0.125
- trainer_out: float32 [2048, 2048], P(None, ('row', 'col')), may hold values from -0.125 to 0.125
- router: bfloat16 [2048, 64], replicated, may hold values from -0.125 to 0.125
- shared_gate: bfloat16 [2048, 2816], P(None, 'col'), may hold values from -0.125 to 0.125
- shared_up: bfloat16 [2048, 2816], P(None, 'col'), may hold values from -0.125 to 0.125
- shared_down: bfloat16 [2816, 2048], P('col'), may hold values from -0.109375 to 0.109375
- expert_gate_up: bfloat16 [128, 2048, 1408], P(('row', 'col')), may hold values from -0.125 to 0.125
- expert_down: bfloat16 [128, 704, 2048], P(('row', 'col')), may hold values from -0.15625 to 0.15625
- lengths: int32 [8], replicated, may hold values from 1 to 2176, as said below
- order: int32 [8], replicated, may hold values from 0 to 7, as said below
- routes: int32 [4096, 6], P('row'), may hold values from 0 to 63, all different within a row; in each aligned block of 256 rows (0 to 255, 256 to 511, ...) at most 40 rows name the same one
Outputs:
- hidden_states: bfloat16 [4096, 2048], P('row', 'col')
- kv_cache: bfloat16 [4096, 1024], P('row', 'col')
- qkv_block: bfloat16 [2048, 4096], P('row', 'col')
- out_block: bfloat16 [2048, 2048], P('col', 'row')
The draws below stay inside these ranges and needn't reach their ends.
Inputs may be any that keep to these rules, and one draw needn't show every extreme that they name: `attn_gain`: positive and not all equal. `lengths`: request 0 has exactly 2176 tokens; every other request has at least one; they sum to 4096. `order`: each request once; request 0 is packed last. `routes`: each row names 6 different experts; in the rows of one device along row (aligned blocks of 256 rows) no expert is named by more than 40 rows, a bound that some block reaches.
All inputs are finite; a program needn't handle non-finite values.
Results may differ from the reference program's by a relative error of at most 0.022.
The reference program's roundings to bfloat16 on the way count: a program that leaves them out, or rounds other values in their place, can miss the bound.
Values may be sent and summed in bfloat16 or wider, within the bound.
No kernel may reach another device: no remote copies, remote signals or barrier semaphores. Data moves between devices by JAX's collectives and lax.ppermute only.
A program may use at most 128 MiB of HBM per device.

```python
import math
import jax
import jax.numpy as jnp
import numpy as np
from jax import lax

D = 2048
HEAD_DIM = 128
EXPERT_FF = 1408
SHARED_FF = 2816
TOP = 6
PROMPTS = 8
TOK_ROW = 256
HEADS = 16
KV_HEADS = 4
EXPERTS = 64
HALF = 704
TOTAL = 4096
PROMPT_MAX = 2176
CAP = 40
N_ROW = 16


def draw_attn_gain(key, part):
    return jax.random.uniform(key, (D,), jnp.float32, 0.5, 1.5)


def draw_lengths(key, part):
    remaining = TOTAL - PROMPT_MAX
    picked = jax.random.permutation(jax.random.fold_in(key, 11), remaining - 1)[:PROMPTS - 2] + 1
    cuts = jnp.sort(picked.astype(jnp.int32))
    edges = jnp.concatenate([jnp.zeros((1,), jnp.int32), cuts, jnp.full((1,), remaining, jnp.int32)])
    others = (edges[1:] - edges[:-1]).astype(jnp.int32)
    return jnp.concatenate([jnp.full((1,), PROMPT_MAX, jnp.int32), others]).astype(jnp.int32)


def draw_order(key, part):
    rest = (jax.random.permutation(jax.random.fold_in(key, 23), PROMPTS - 1) + 1).astype(jnp.int32)
    return jnp.concatenate([rest, jnp.zeros((1,), jnp.int32)]).astype(jnp.int32)


def block_scale(key, shape, split, least, high):
    def one(axis_at, parts):
        heights = jax.random.uniform(jax.random.fold_in(jax.random.fold_in(key, 6), axis_at), (parts,), jnp.float32, least / len(split), high / len(split))
        return jnp.repeat(jnp.exp(heights), shape[axis_at] // parts).reshape((-1,) + (1,) * (len(shape) - axis_at - 1))

    level = one(*split[0])
    for cut in split[1:]:
        level = level * one(*cut)
    return level


def deal_out(own_key, own, number, rows, amount, top, most, lean):
    sequence = jax.random.permutation(own_key, amount)
    packed, common = shares(amount, rows * top, most, lean, True), shares(amount, rows * top, most, lean, False)
    places = jnp.arange(amount)

    def named(sizes, turn):
        used = int((sizes > 0).sum())
        fixed = max(1, used // 4)
        passed = fixed + (places - fixed + turn * (used - fixed)) % max(1, amount - fixed)
        return jnp.zeros((amount,), jnp.int32).at[sequence[jnp.where(places < fixed, places, passed)]].set(jnp.asarray(sizes, jnp.int32))

    sizes = jnp.where(number % 4 == 0, named(packed, number // 4), named(common, number - number // 4 - 1))
    mixed = jax.random.permutation(jax.random.fold_in(own, 3), amount)
    donor, sink = mixed[0:amount // 2 * 2:2], mixed[1:amount // 2 * 2:2]
    margin = jnp.minimum(sizes[donor] - 1, most - sizes[sink]) // 2
    margin = jnp.where((donor == sequence[0]) | (sink == sequence[0]) | (sizes[sink] == 0), 0, jnp.maximum(margin, 0))
    passed = jax.random.randint(jax.random.fold_in(own, 4), (amount // 2,), 0, 1 << 20) % (margin + 1)
    sizes = sizes.at[donor].add(-passed).at[sink].add(passed)
    members = jnp.searchsorted(jnp.cumsum(sizes), jnp.arange(rows * top), side="right").astype(jnp.int32)
    listing = members.reshape(top, rows).T
    listing = listing[jax.random.permutation(jax.random.fold_in(own, 1), rows)]
    turn = jax.random.randint(jax.random.fold_in(own, 2), (rows, 1), 0, top)
    return jnp.take_along_axis(listing, (jnp.arange(top)[None, :] + turn) % top, axis=1)


def shares(count, total, limit, slope, full):
    portions = [(1 << 20) // math.isqrt(standing ** slope) + 1 for standing in range(1, count + 1)]
    largest = limit if full else min(limit, max(-(-total // count), total * portions[0] // sum(portions)))
    least = 1 if total - largest >= count - 1 else 0
    holding, surplus = [largest] + [least] * (count - 1), total - largest - least * (count - 1)
    while surplus > 0:
        candidates = [i for i in range(1, count) if holding[i] < largest] or [i for i in range(1, count) if holding[i] < limit]
        whole, left = sum([portions[i] for i in candidates]), surplus
        for i in candidates:
            addition = min(limit - holding[i], max(1, left * portions[i] // whole), surplus)
            holding[i] = holding[i] + addition
            surplus = surplus - addition
    return np.array(holding)


def noise(rng, extent, deviation, limit, split=(), held_as=jnp.bfloat16):
    values = deviation * jax.random.normal(rng, extent, jnp.float32)
    if split:
        values = values * block_scale(rng, extent, split, -0.22, 0.18)
    return jnp.clip(values, -limit, limit).astype(held_as)


def setup_inputs(seed: int = 0) -> dict:
    splits = jax.random.split(jax.random.key(seed), 15)
    tokens = noise(splits[0], (TOTAL, D), 1.0, 6.0, ((0, 16), (1, 8)))
    attn_gain = draw_attn_gain(jax.random.fold_in(splits[14], 71), 0)
    mlp_gain = jnp.clip(1.0 + 0.1 * jax.random.normal(splits[2], (D,), jnp.float32), 0.5, 1.5)
    trainer_qkv = noise(splits[3], (D, (HEADS + 2 * KV_HEADS) * HEAD_DIM), D ** -0.5, 0.125, ((0, 128),), jnp.float32)
    trainer_out = noise(splits[4], (HEADS * HEAD_DIM, D), (HEADS * HEAD_DIM) ** -0.5, 0.125, ((1, 128),), jnp.float32)
    router = noise(splits[5], (D, EXPERTS), D ** -0.5, 0.125)
    shared_gate = noise(splits[6], (D, SHARED_FF), D ** -0.5, 0.125, ((1, 8),))
    shared_up = noise(splits[7], (D, SHARED_FF), D ** -0.5, 0.125, ((1, 8),))
    shared_down = noise(splits[8], (SHARED_FF, D), SHARED_FF ** -0.5, 0.109375, ((0, 8),))
    expert_gate_up = noise(splits[9], (2 * EXPERTS, D, 2 * HALF), D ** -0.5, 0.125, ((0, 128),))
    expert_down = noise(splits[10], (2 * EXPERTS, HALF, D), EXPERT_FF ** -0.5, 0.15625, ((0, 128),))
    lengths = draw_lengths(jax.random.fold_in(splits[14], 71), 0)
    order = draw_order(jax.random.fold_in(splits[14], 71), 0)
    routes_keys = jax.random.split(jax.random.fold_in(splits[13], 1), TOTAL // TOK_ROW)
    routes_turns = jax.random.permutation(jax.random.fold_in(splits[13], 3), TOTAL // TOK_ROW)
    routes = jax.vmap(lambda own, number: deal_out(jax.random.fold_in(splits[13], 2), own, number, TOK_ROW, EXPERTS, TOP, CAP, 1))(routes_keys, routes_turns).reshape((TOTAL, TOP))
    return {"tokens": tokens, "attn_gain": attn_gain, "mlp_gain": mlp_gain, "trainer_qkv": trainer_qkv, "trainer_out": trainer_out, "router": router, "shared_gate": shared_gate, "shared_up": shared_up, "shared_down": shared_down, "expert_gate_up": expert_gate_up, "expert_down": expert_down, "lengths": lengths, "order": order, "routes": routes}


epsilon = 1e-06
rope_base = 600000.0
masked_score = -1e+30

def prompt_tables(lengths, order, first, height):
    prompt_ids = jnp.arange(lengths.shape[0], dtype=jnp.int32)
    picked = order[:, None] == prompt_ids[None, :]
    packed_len = lax.optimization_barrier(jnp.sum(jnp.where(picked, lengths[None, :], 0), axis=1)).astype(jnp.int32)
    packed_end = jnp.cumsum(packed_len).astype(jnp.int32)
    packed_start = (packed_end - packed_len).astype(jnp.int32)
    request_start = (jnp.cumsum(lengths) - lengths).astype(jnp.int32)
    positions = (first + jnp.arange(height, dtype=jnp.int32)).astype(jnp.int32)
    segment = lax.optimization_barrier(jnp.sum((positions[:, None] >= packed_end[None, :]).astype(jnp.int32), axis=1)).astype(jnp.int32)
    onehot = segment[:, None] == prompt_ids[None, :]
    within = (positions - lax.optimization_barrier(jnp.sum(jnp.where(onehot, packed_start[None, :], 0), axis=1))).astype(jnp.int32)
    request = lax.optimization_barrier(jnp.sum(jnp.where(onehot, order[None, :], 0), axis=1)).astype(jnp.int32)
    offset = lax.optimization_barrier(jnp.sum(jnp.where(request[:, None] == prompt_ids[None, :], request_start[None, :], 0), axis=1))
    return (segment, within, (within + offset).astype(jnp.int32))

def rms_scale(values, gain):
    wide = values.astype(jnp.float32)
    return wide * lax.rsqrt(lax.optimization_barrier(jnp.mean(wide * wide, axis=-1, keepdims=True)) + epsilon) * gain

def rotary(values, within):
    half_dim = values.shape[-1] // 2
    inverse = rope_base ** (-jnp.arange(half_dim, dtype=jnp.float32) * 2.0 / values.shape[-1])
    angles = within.astype(jnp.float32)[:, None] * inverse[None, :]
    cosine = jnp.cos(angles)
    sine_part = jnp.sin(angles)
    lower = values[..., :half_dim]
    upper = values[..., half_dim:]
    return jnp.concatenate([lower * cosine - upper * sine_part, upper * cosine + lower * sine_part], axis=-1)

def server_columns(trainer_rows, groups):
    height = trainer_rows.shape[0]
    kv_count = groups // 2
    query_part = trainer_rows[:, :2 * groups * HEAD_DIM].reshape(height, groups, 2 * HEAD_DIM)
    key_part = trainer_rows[:, 2 * groups * HEAD_DIM:(2 * groups + kv_count) * HEAD_DIM].reshape(height, kv_count, 1, HEAD_DIM)
    value_part = trainer_rows[:, (2 * groups + kv_count) * HEAD_DIM:].reshape(height, kv_count, 1, HEAD_DIM)
    key_part = jnp.broadcast_to(key_part, (height, kv_count, 2, HEAD_DIM)).reshape(height, groups, HEAD_DIM)
    value_part = jnp.broadcast_to(value_part, (height, kv_count, 2, HEAD_DIM)).reshape(height, groups, HEAD_DIM)
    joined = jnp.concatenate([query_part, key_part, value_part], axis=2)
    return joined.reshape(height, groups * 4 * HEAD_DIM).astype(jnp.bfloat16)

def reference(tokens, attn_gain, mlp_gain, trainer_qkv, trainer_out, router, shared_gate, shared_up, shared_down, expert_gate_up, expert_down, lengths, order, routes):
    groups = 2 * KV_HEADS
    qkv_block = server_columns(trainer_qkv, groups)
    out_block = trainer_out.astype(jnp.bfloat16)
    segment, within, dest = prompt_tables(lengths, order, 0, TOTAL)
    normed = rms_scale(tokens, attn_gain).astype(jnp.bfloat16)
    projected = jnp.dot(normed, qkv_block, preferred_element_type=jnp.float32).reshape(TOTAL, groups, 4, HEAD_DIM)
    queries = projected[:, :, 0:2, :].reshape(TOTAL, HEADS, HEAD_DIM).transpose(1, 0, 2)
    queries = rotary(queries, within).astype(jnp.bfloat16)
    key_rows = rotary(projected[:, 0::2, 2, :].transpose(1, 0, 2), within).astype(jnp.bfloat16)
    value_rows = projected[:, 0::2, 3, :].transpose(1, 0, 2).astype(jnp.bfloat16)
    kv_cache = jnp.stack([key_rows, value_rows], axis=1).transpose(2, 0, 1, 3).reshape(TOTAL, 2 * KV_HEADS * HEAD_DIM)
    per_group = HEADS // KV_HEADS
    key_wide = key_rows.astype(jnp.float32)
    value_wide = value_rows.astype(jnp.float32)
    key_positions = jnp.arange(TOTAL, dtype=jnp.int32)

    def attend(block_index):
        block_start = (block_index * TOK_ROW).astype(jnp.int32)
        query_block = lax.dynamic_slice_in_dim(queries, block_start, TOK_ROW, 1).astype(jnp.float32)
        query_block = query_block.reshape(KV_HEADS, per_group, TOK_ROW, HEAD_DIM)
        query_seg = lax.dynamic_slice_in_dim(segment, block_start, TOK_ROW, 0)
        query_pos = block_start + jnp.arange(TOK_ROW, dtype=jnp.int32)
        allowed = (segment[None, :] == query_seg[:, None]) & (key_positions[None, :] <= query_pos[:, None])
        scores = jnp.einsum('gqrd,gkd->gqrk', query_block, key_wide) * HEAD_DIM ** (-0.5)
        scores = jnp.where(allowed, scores, masked_score)
        row_peak = lax.optimization_barrier(jnp.max(scores, axis=-1, keepdims=True))
        numerators = jnp.where(allowed, jnp.exp(scores - row_peak), 0.0)
        denominator = lax.optimization_barrier(jnp.sum(numerators, axis=-1))
        rounded = lax.optimization_barrier(numerators.astype(jnp.bfloat16))
        summed = jnp.einsum('gqrk,gkd->gqrd', rounded.astype(jnp.float32), value_wide) / denominator[..., None]
        summed = summed.reshape(HEADS, TOK_ROW, HEAD_DIM).transpose(1, 0, 2)
        return summed.reshape(TOK_ROW, HEADS * HEAD_DIM).astype(jnp.bfloat16)
    attended = lax.map(attend, jnp.arange(N_ROW, dtype=jnp.int32)).reshape(TOTAL, HEADS * HEAD_DIM)
    resid = (tokens.astype(jnp.float32) + jnp.dot(attended, out_block, preferred_element_type=jnp.float32)).astype(jnp.bfloat16)
    mlp_in = rms_scale(resid, mlp_gain).astype(jnp.bfloat16)
    logits = jnp.dot(mlp_in, router, preferred_element_type=jnp.float32)
    router_probs = jax.nn.softmax(logits, axis=-1)
    expert_ids = jnp.arange(EXPERTS, dtype=jnp.int32)
    chosen = lax.optimization_barrier(jnp.sum(jnp.where(routes[:, :, None] == expert_ids[None, None, :], router_probs[:, None, :], 0.0), axis=-1))
    route_weight = (chosen / lax.optimization_barrier(jnp.sum(chosen, axis=-1, keepdims=True))).astype(jnp.bfloat16)
    shared_hidden = (jax.nn.silu(jnp.dot(mlp_in, shared_gate, preferred_element_type=jnp.float32)) * jnp.dot(mlp_in, shared_up, preferred_element_type=jnp.float32)).astype(jnp.bfloat16)
    shared_out = jnp.dot(shared_hidden, shared_down, preferred_element_type=jnp.float32)
    slots = N_ROW * CAP
    weight_wide = route_weight.astype(jnp.float32)

    def one_expert(running, expert):
        matches = routes == expert
        member = jnp.any(matches, axis=1)
        gathered_weight = lax.optimization_barrier(jnp.sum(jnp.where(matches, weight_wide, 0.0), axis=1))
        slot_index = jnp.nonzero(member, size=slots, fill_value=0)[0].astype(jnp.int32)
        usable = jnp.arange(slots, dtype=jnp.int32) < jnp.sum(member.astype(jnp.int32))
        picked = mlp_in[slot_index]
        summed = jnp.zeros((slots, D), jnp.float32)
        for half_index in range(2):
            slab_index = (2 * expert + half_index).astype(jnp.int32)
            gate_up = jnp.dot(picked, lax.dynamic_index_in_dim(expert_gate_up, slab_index, 0, keepdims=False), preferred_element_type=jnp.float32)
            hidden = (jax.nn.silu(gate_up[:, :HALF]) * gate_up[:, HALF:]).astype(jnp.bfloat16)
            partial_value = jnp.dot(hidden, lax.dynamic_index_in_dim(expert_down, slab_index, 0, keepdims=False), preferred_element_type=jnp.float32)
            summed = summed + lax.optimization_barrier(partial_value.astype(jnp.bfloat16)).astype(jnp.float32)
        contrib = jnp.where(usable[:, None], gathered_weight[slot_index][:, None] * summed, 0.0)
        return (running.at[slot_index].add(contrib), None)
    routed, _ = lax.scan(one_expert, jnp.zeros((TOTAL, D), jnp.float32), expert_ids)
    layer_out = (resid.astype(jnp.float32) + shared_out + routed).astype(jnp.bfloat16)
    hidden_states = jnp.zeros_like(layer_out).at[dest].set(layer_out)
    return (hidden_states, kv_cache, qkv_block, out_block)
```

```python
import jax
import jax.numpy as jnp
from jax import lax
from jax.sharding import Mesh
from jax.sharding import PartitionSpec as P

D = 2048
HEAD_DIM = 128
TOP = 6
FIRST_LONG = 1920

ROW = ("zh", "y", "k")
COL = ("zl", "x")

epsilon = 1e-06
rope_base = 600000.0
masked_score = -1e30


def prompt_tables(lengths, order, positions):
    prompt_ids = jnp.arange(lengths.shape[0], dtype=jnp.int32)
    picked = order[:, None] == prompt_ids[None, :]
    packed_len = jnp.sum(jnp.where(picked, lengths[None, :], 0), axis=1)
    packed_end = jnp.cumsum(packed_len)
    packed_start = packed_end - packed_len
    request_start = jnp.cumsum(lengths) - lengths
    segment = jnp.sum((positions[:, None] >= packed_end[None, :]).astype(jnp.int32), axis=1)
    onehot = segment[:, None] == prompt_ids[None, :]
    within = positions - jnp.sum(jnp.where(onehot, packed_start[None, :], 0), axis=1)
    request = jnp.sum(jnp.where(onehot, order[None, :], 0), axis=1)
    offset = jnp.sum(
        jnp.where(request[:, None] == prompt_ids[None, :], request_start[None, :], 0), axis=1
    )
    return (segment, within, within + offset)


def rms_scale(values, gain):
    wide = values.astype(jnp.float32)
    return wide * lax.rsqrt(jnp.mean(wide * wide, axis=-1, keepdims=True) + epsilon) * gain


def rotary(values, within):
    half_dim = values.shape[-1] // 2
    inverse = rope_base ** (-jnp.arange(half_dim, dtype=jnp.float32) * 2.0 / values.shape[-1])
    angles = within.astype(jnp.float32)[:, None] * inverse[None, :]
    cosine = jnp.cos(angles)
    sine_part = jnp.sin(angles)
    lower = values[..., :half_dim]
    upper = values[..., half_dim:]
    return jnp.concatenate(
        [lower * cosine - upper * sine_part, upper * cosine + lower * sine_part], axis=-1
    )


def server_columns(trainer_rows, groups):
    height = trainer_rows.shape[0]
    kv_count = groups // 2
    query_part = trainer_rows[:, : 2 * groups * HEAD_DIM].reshape(height, groups, 2 * HEAD_DIM)
    key_part = trainer_rows[:, 2 * groups * HEAD_DIM : (2 * groups + kv_count) * HEAD_DIM].reshape(
        height, kv_count, 1, HEAD_DIM
    )
    value_part = trainer_rows[:, (2 * groups + kv_count) * HEAD_DIM :].reshape(
        height, kv_count, 1, HEAD_DIM
    )
    key_part = jnp.broadcast_to(key_part, (height, kv_count, 2, HEAD_DIM)).reshape(
        height, groups, HEAD_DIM
    )
    value_part = jnp.broadcast_to(value_part, (height, kv_count, 2, HEAD_DIM)).reshape(
        height, groups, HEAD_DIM
    )
    joined = jnp.concatenate([query_part, key_part, value_part], axis=2)
    return joined.reshape(height, groups * 4 * HEAD_DIM).astype(jnp.bfloat16)


def to_all(block, axes, count):
    copies = jnp.broadcast_to(block[None], (count,) + block.shape)
    return lax.all_to_all(copies, axes, 0, 0, tiled=True)


def core_swap(block):
    return lax.ppermute(block, "k", [(0, 1), (1, 0)])


def col_gather(block, col_index):
    count = 8
    height, width = block.shape
    whole = jnp.zeros((height, count * width), block.dtype)
    for step in range(count):
        if step == 0:
            piece = block
        else:
            piece = lax.ppermute(block, COL, [(i, i ^ step) for i in range(count)])
        whole = lax.dynamic_update_slice(whole, piece, (0, (col_index ^ step) * width))
    return whole


def on_device(
    tokens,
    attn_gain,
    mlp_gain,
    trainer_qkv,
    trainer_out,
    router,
    shared_gate,
    shared_up,
    shared_down,
    expert_gate_up,
    expert_down,
    lengths,
    order,
    routes,
):
    tok_rows = tokens.shape[0]
    row_count, col_count = 16, 8
    zh_index = lax.axis_index("zh")
    y_index = lax.axis_index("y")
    k_index = lax.axis_index("k")
    row_index = lax.axis_index(ROW)
    col_index = lax.axis_index(COL)
    first = row_index * tok_rows
    local = jnp.arange(tok_rows, dtype=jnp.int32)

    qkv_block = lax.all_to_all(
        server_columns(trainer_qkv, col_count).reshape(16, col_count, 512).transpose(1, 0, 2),
        COL, 0, 0, tiled=True,
    ).reshape(128, 512)
    full_tokens = col_gather(tokens, col_index)
    qkv_mine = to_all(qkv_block, ("zh", "y"), 8)
    qkv_other = core_swap(qkv_mine)

    out_block = lax.all_to_all(
        trainer_out.astype(jnp.bfloat16).reshape(col_count, 256, 16), COL, 0, 0, tiled=True
    ).transpose(1, 0, 2).reshape(256, 128)
    out_mine = to_all(out_block, ("zh", "y"), 8)
    out_other = core_swap(out_mine)

    seg_query, within_query, _ = prompt_tables(lengths, order, first + local)
    normed = rms_scale(full_tokens, attn_gain).astype(jnp.bfloat16)
    normed4 = normed.reshape(tok_rows, 8, 2, 128)
    mine_in = jnp.where(k_index == 0, normed4[:, :, 0], normed4[:, :, 1]).reshape(tok_rows, 1024)
    other_in = jnp.where(k_index == 0, normed4[:, :, 1], normed4[:, :, 0]).reshape(tok_rows, 1024)
    projected = jnp.dot(
        mine_in, qkv_mine.reshape(1024, 512), preferred_element_type=jnp.float32
    ) + jnp.dot(other_in, qkv_other.reshape(1024, 512), preferred_element_type=jnp.float32)
    queries = projected[:, : 2 * HEAD_DIM].reshape(tok_rows, 2, HEAD_DIM).transpose(1, 0, 2)
    queries = rotary(queries, within_query).astype(jnp.bfloat16)
    key_rows = rotary(projected[:, 2 * HEAD_DIM : 3 * HEAD_DIM], within_query).astype(jnp.bfloat16)
    value_rows = projected[:, 3 * HEAD_DIM :].astype(jnp.bfloat16)
    cache_out = jnp.where(col_index % 2 == 0, key_rows, value_rows)

    kv_rows = jnp.concatenate([key_rows, value_rows], axis=1)
    tail = kv_rows[128:]
    head_sent = sum(lax.ppermute(tail, ROW, [(7, to)]) for to in (9, 11, 13, 15))
    kv_mine = to_all(kv_rows, "y", 4)
    kv_other = core_swap(kv_mine)
    kv_head = head_sent + core_swap(head_sent)
    kv_all = jnp.concatenate(
        [kv_mine.reshape(1024, 256), kv_other.reshape(1024, 256), kv_head], axis=0
    )
    span = jnp.arange(1024, dtype=jnp.int32)
    base_pos = zh_index * 2048 + (span // 256) * 512 + span % 256
    head_pos = FIRST_LONG + jnp.arange(128, dtype=jnp.int32)
    key_pos = jnp.concatenate(
        [
            base_pos + k_index * 256,
            base_pos + (1 - k_index) * 256,
            jnp.where(zh_index == 1, head_pos, jnp.int32(1 << 20)),
        ]
    )
    seg_key, _, _ = prompt_tables(lengths, order, key_pos)
    query_pos = first + local
    allowed = (seg_key[None, :] == seg_query[:, None]) & (key_pos[None, :] <= query_pos[:, None])
    scale = HEAD_DIM ** (-0.5)
    scores = (
        jnp.einsum(
            "hqd,kd->hqk", queries, kv_all[:, :HEAD_DIM], preferred_element_type=jnp.float32
        )
        * scale
    )
    scores = jnp.where(allowed[None], scores, masked_score)
    peak = jnp.max(scores, axis=2)
    numerators = jnp.where(allowed[None], jnp.exp(scores - peak[..., None]), 0.0)
    denominator = jnp.sum(numerators, axis=2)
    summed = jnp.einsum(
        "hqk,kd->hqd",
        numerators.astype(jnp.bfloat16),
        kv_all[:, HEAD_DIM:],
        preferred_element_type=jnp.float32,
    )
    attended = (
        (summed / denominator[..., None])
        .transpose(1, 0, 2)
        .reshape(tok_rows, 2 * HEAD_DIM)
        .astype(jnp.bfloat16)
    )
    terms = jnp.concatenate(
        [
            jnp.einsum("th,fhn->ftn", attended, out_mine, preferred_element_type=jnp.float32),
            jnp.einsum("th,fhn->ftn", attended, out_other, preferred_element_type=jnp.float32),
        ],
        axis=2,
    ).astype(jnp.bfloat16)
    got = lax.all_to_all(terms, COL, 0, 0, tiled=True)
    attn_sum = jnp.sum(got.astype(jnp.float32), axis=0)
    attn_part = jnp.where(k_index == 0, attn_sum, jnp.roll(attn_sum, 128, axis=1))
    resid = (tokens.astype(jnp.float32) + attn_part).astype(jnp.bfloat16)

    full_resid = col_gather(resid, col_index)
    mlp_in = rms_scale(full_resid, mlp_gain).astype(jnp.bfloat16)
    logits = jnp.dot(mlp_in, router, preferred_element_type=jnp.float32)
    router_probs = jax.nn.softmax(logits, axis=-1)
    n_experts = row_count * col_count // 2
    expert_ids = jnp.arange(n_experts, dtype=jnp.int32)
    chosen = jnp.sum(
        jnp.where(routes[:, :, None] == expert_ids[None, None, :], router_probs[:, None, :], 0.0),
        axis=-1,
    )
    route_weight = (chosen / jnp.sum(chosen, axis=-1, keepdims=True)).astype(jnp.bfloat16)
    shared_hidden = (
        jax.nn.silu(jnp.dot(mlp_in, shared_gate, preferred_element_type=jnp.float32))
        * jnp.dot(mlp_in, shared_up, preferred_element_type=jnp.float32)
    ).astype(jnp.bfloat16)
    capacity = 40
    targets = jnp.arange(row_count, dtype=jnp.int32) * (col_count // 2) + col_index // 2
    matches = routes[:, :, None] == targets[None, None, :]
    member = jnp.any(matches, axis=1)
    slot_of = jnp.cumsum(member.astype(jnp.int32), axis=0) - 1
    chosen_weight = jnp.sum(
        jnp.where(matches, route_weight[:, :, None].astype(jnp.float32), 0.0), axis=1
    )
    placing = member[:, :, None] & (
        slot_of[:, :, None] == jnp.arange(capacity, dtype=jnp.int32)[None, None, :]
    )
    picker = placing.astype(jnp.bfloat16).reshape(tok_rows, row_count * capacity)
    combiner = (
        (placing.astype(jnp.float32) * chosen_weight[:, :, None])
        .astype(jnp.bfloat16)
        .reshape(tok_rows, row_count * capacity)
    )
    outgoing = jnp.einsum("ts,td->sd", picker, mlp_in, preferred_element_type=jnp.float32).astype(
        jnp.bfloat16
    )
    outgoing = outgoing.reshape(row_count, capacity, D)
    gate_up_slab = expert_gate_up[0]
    down_slab = expert_down[0]
    half_units = down_slab.shape[0]
    arrived = lax.all_to_all(outgoing, ROW, split_axis=0, concat_axis=0, tiled=True)
    flat = arrived.reshape(-1, D)
    gate_up = jnp.dot(flat, gate_up_slab, preferred_element_type=jnp.float32)
    hidden = (jax.nn.silu(gate_up[:, :half_units]) * gate_up[:, half_units:]).astype(jnp.bfloat16)
    result = (
        jnp.dot(hidden, down_slab, preferred_element_type=jnp.float32)
        .astype(jnp.bfloat16)
        .reshape(arrived.shape)
    )
    came_back = lax.all_to_all(result, ROW, split_axis=0, concat_axis=0, tiled=True)
    came_back = came_back.reshape(row_count * capacity, D)
    parts = jnp.stack(
        [
            jnp.dot(
                combiner, came_back[:, f * 256 : (f + 1) * 256], preferred_element_type=jnp.float32
            )
            + jnp.dot(
                shared_hidden,
                shared_down[:, f * 256 : (f + 1) * 256],
                preferred_element_type=jnp.float32,
            )
            for f in range(col_count)
        ]
    ).astype(jnp.bfloat16)
    layer_got = lax.all_to_all(parts, COL, 0, 0, tiled=True)
    layer_part = jnp.sum(layer_got.astype(jnp.float32), axis=0)
    layer_out = (resid.astype(jnp.float32) + layer_part).astype(jnp.bfloat16)

    received = []
    for step in range(4):
        pairs = [(s, 4 + (s + step) % 4) for s in range(4)]
        if step == 0:
            pairs += [(4 + s, s) for s in range(4)]
        received.append(lax.ppermute(layer_out, ("zh", "y"), pairs))
    late = lax.ppermute(
        layer_out[128:], ROW, [(7 + i, i) for i in range(0, 8, 2)] + [(15, 8)]
    )
    mine_rows = jnp.concatenate(received, axis=0)
    other_rows = core_swap(mine_rows)
    sources = jnp.concatenate([mine_rows, other_rows, late], axis=0)
    step_of = span // 256
    from_row = jnp.where(
        zh_index == 1,
        ((y_index - step_of) % 4) * 2,
        jnp.where(step_of == 0, 8 + y_index * 2, jnp.int32(1 << 12)),
    )
    late_from = jnp.where(
        k_index == 1, 1 << 12, jnp.where(zh_index == 0, row_index + 7, jnp.where(row_index == 8, 15, 1 << 12))
    )
    source_pos = jnp.concatenate(
        [
            (from_row + k_index) * 256 + span % 256,
            (from_row + 1 - k_index) * 256 + span % 256,
            late_from * 256 + 128 + jnp.arange(128, dtype=jnp.int32),
        ]
    )
    _, _, dest = prompt_tables(lengths, order, source_pos)
    dest = jnp.where(source_pos < row_count * tok_rows, dest, -1)
    mover = (dest[None, :] == (first + local)[:, None]).astype(jnp.bfloat16)
    hidden_states = jnp.dot(mover, sources, preferred_element_type=jnp.float32).astype(jnp.bfloat16)
    return (hidden_states, cache_out, qkv_block, out_block)


def solution(mesh):
    fine = Mesh(mesh.devices.reshape(2, 4, 2, 2, 4), ROW + COL)
    in_specs = (
        P(ROW, COL),
        P(),
        P(),
        P(ROW + COL, None),
        P(None, ROW + COL),
        P(),
        P(None, COL),
        P(None, COL),
        P(COL, None),
        P(ROW + COL, None, None),
        P(ROW + COL, None, None),
        P(),
        P(),
        P(ROW, None),
    )
    out_specs = (P(ROW, COL), P(ROW, COL), P(ROW, COL), P(COL, ROW))
    return jax.shard_map(
        on_device, mesh=fine, in_specs=in_specs, out_specs=out_specs, check_vma=False
    )
```

```python
import jax
import jax.numpy as jnp
from jax import lax
from jax.experimental import pallas as pl
from jax.experimental.pallas import tpu as pltpu
from jax.sharding import Mesh
from jax.sharding import PartitionSpec as P

D = 2048
HEAD_DIM = 128
TOP = 6
FIRST_LONG = 1920

ROW = ("zh", "y", "k")
COL = ("zl", "x")

epsilon = 1e-06
rope_base = 600000.0
masked_score = -1e30


def prompt_tables(lengths, order, positions):
    prompt_ids = jnp.arange(lengths.shape[0], dtype=jnp.int32)
    picked = order[:, None] == prompt_ids[None, :]
    packed_len = jnp.sum(jnp.where(picked, lengths[None, :], 0), axis=1)
    packed_end = jnp.cumsum(packed_len)
    packed_start = packed_end - packed_len
    request_start = jnp.cumsum(lengths) - lengths
    segment = jnp.sum((positions[:, None] >= packed_end[None, :]).astype(jnp.int32), axis=1)
    onehot = segment[:, None] == prompt_ids[None, :]
    within = positions - jnp.sum(jnp.where(onehot, packed_start[None, :], 0), axis=1)
    request = jnp.sum(jnp.where(onehot, order[None, :], 0), axis=1)
    offset = jnp.sum(
        jnp.where(request[:, None] == prompt_ids[None, :], request_start[None, :], 0), axis=1
    )
    return (segment, within, within + offset)


def rms_scale(values, gain):
    wide = values.astype(jnp.float32)
    return wide * lax.rsqrt(jnp.mean(wide * wide, axis=-1, keepdims=True) + epsilon) * gain


def rotary_tables(within, size):
    half_dim = size // 2
    inverse = rope_base ** (-jnp.arange(half_dim, dtype=jnp.float32) * 2.0 / size)
    angles = within.astype(jnp.float32)[:, None] * inverse[None, :]
    cosine = jnp.cos(angles)
    sine_part = jnp.sin(angles)
    return (
        jnp.concatenate([cosine, cosine], axis=1),
        jnp.concatenate([-sine_part, sine_part], axis=1),
    )


def core_swap(block):
    return lax.ppermute(block, "k", [(0, 1), (1, 0)])


def col_gather(block):
    copies = jnp.broadcast_to(block[None], (8,) + block.shape)
    return lax.all_to_all(copies, COL, 0, 0, tiled=True)


def projection_kernel(came_ref, mine_ref, other_ref, gain_ref, cos_ref, sin_ref, q_ref, kv_ref):
    core = lax.axis_index("k")
    squares = jnp.zeros((256, HEAD_DIM), jnp.float32)
    for member in range(8):
        for part in range(2):
            x = came_ref[member, 64 + part * 256 : 320 + part * 256, :].astype(jnp.float32)
            squares += x * x
    mean = jnp.sum(squares, axis=1, keepdims=True) * (1.0 / D)
    level = lax.rsqrt(mean + epsilon)
    total = jnp.zeros((256, 4 * HEAD_DIM), jnp.float32)
    for member in range(8):
        inputs, weights = [], []
        for part, ref in ((core, mine_ref), (1 - core, other_ref)):
            at = pl.multiple_of(64 + part * 256, 64)
            x = came_ref[member, pl.ds(at, 256), :].astype(jnp.float32)
            gain = gain_ref[pl.ds(2 * member + part, 1), :]
            inputs.append((x * level * gain).astype(jnp.bfloat16))
            weights.append(
                jnp.concatenate(
                    [ref[member, h * HEAD_DIM : (h + 1) * HEAD_DIM, :] for h in range(4)], axis=1
                )
            )
        total += jnp.dot(
            jnp.concatenate(inputs, axis=1),
            jnp.concatenate(weights, axis=0),
            preferred_element_type=jnp.float32,
        )
    cosine = cos_ref[...]
    sine_part = sin_ref[...]
    for h in range(4):
        part = total[:, h * HEAD_DIM : (h + 1) * HEAD_DIM]
        if h < 3:
            part = part * cosine + pltpu.roll(part, HEAD_DIM // 2, 1) * sine_part
        part = part.astype(jnp.bfloat16)
        if h < 2:
            q_ref[h] = part
        else:
            kv_ref[:, (h - 2) * HEAD_DIM : (h - 1) * HEAD_DIM] = part


def in_vmem(count):
    return [pl.BlockSpec(memory_space=pltpu.VMEM)] * count


def projection(came, mine, other, gain, cosine, sine_part):
    return pl.pallas_call(
        projection_kernel,
        in_specs=in_vmem(6),
        out_shape=(
            jax.ShapeDtypeStruct((2, 256, HEAD_DIM), jnp.bfloat16),
            jax.ShapeDtypeStruct((256, 2 * HEAD_DIM), jnp.bfloat16),
        ),
        name="projection",
    )(came, mine, other, gain, cosine, sine_part)


def attention_kernel(
    q_ref, mine_ref, other_ref, head_ref, start_ref, out_mine_ref, out_other_ref, terms_ref, s_ref
):
    half, core = lax.axis_index("zh"), lax.axis_index("k")
    first = half * 2048 + lax.axis_index("y") * 512 + core * 256
    scale = HEAD_DIM ** (-0.5)
    query_pos = first + lax.broadcasted_iota(jnp.int32, (256, 1), 0)
    start = start_ref[...]
    blocks = []
    for y in range(4):
        blocks.append((mine_ref, y, half * 2048 + y * 512 + core * 256, 256))
        blocks.append((other_ref, y, half * 2048 + y * 512 + (1 - core) * 256, 256))
    blocks.append((head_ref, None, jnp.where(half == 1, FIRST_LONG, 1 << 20), 128))

    def piece(ref, index, lanes):
        return ref[:, lanes] if index is None else ref[index, :, lanes]

    heads = []
    for h in range(2):
        query = q_ref[h]
        top = jnp.full((256, 128), masked_score, jnp.float32)
        at = 0
        for ref, index, pos, height in blocks:
            keys = piece(ref, index, slice(0, HEAD_DIM))
            scores = lax.dot_general(
                query, keys, (((1,), (1,)), ((), ())), preferred_element_type=jnp.float32
            ) * scale
            key_pos = pos + lax.broadcasted_iota(jnp.int32, (1, height), 1)
            allowed = (key_pos >= start) & (key_pos <= query_pos)
            scores = jnp.where(allowed, scores, masked_score)
            s_ref[:, at : at + height] = scores
            for lane in range(0, height, 128):
                top = jnp.maximum(top, scores[:, lane : lane + 128])
            at += height
        peak = jnp.max(top, axis=1, keepdims=True)
        sums = jnp.zeros((256, 128), jnp.float32)
        total = jnp.zeros((256, HEAD_DIM), jnp.float32)
        at = 0
        for ref, index, pos, height in blocks:
            numerators = jnp.exp(s_ref[:, at : at + height] - peak)
            for lane in range(0, height, 128):
                sums += numerators[:, lane : lane + 128]
            total += jnp.dot(
                numerators.astype(jnp.bfloat16),
                piece(ref, index, slice(HEAD_DIM, 2 * HEAD_DIM)),
                preferred_element_type=jnp.float32,
            )
            at += height
        heads.append((total / jnp.sum(sums, axis=1, keepdims=True)).astype(jnp.bfloat16))
    attended = jnp.concatenate(heads, axis=1)
    for f in range(8):
        mine = out_mine_ref[f, 512:768, :]
        other = out_other_ref[f, 512:768, :]
        low = jnp.where(core == 0, mine, other)
        high = jnp.where(core == 0, other, mine)
        terms_ref[f] = jnp.dot(
            attended, jnp.concatenate([low, high], axis=1), preferred_element_type=jnp.float32
        ).astype(jnp.bfloat16)


def attention(queries, mine, other, head, start, out_mine, out_other):
    return pl.pallas_call(
        attention_kernel,
        in_specs=in_vmem(7),
        out_shape=jax.ShapeDtypeStruct((8, 256, 256), jnp.bfloat16),
        scratch_shapes=[pltpu.VMEM((256, 2176), jnp.float32)],
        name="attention",
    )(queries, mine, other, head, start, out_mine, out_other)


def dispatch_kernel(resid_ref, gain_ref, slots_ref, mlp_ref, out_ref):
    squares = jnp.zeros((256, 256), jnp.float32)
    for f in range(8):
        x = resid_ref[f].astype(jnp.float32)
        squares += x * x
    level = lax.rsqrt(jnp.sum(squares, axis=1, keepdims=True) * (1.0 / D) + epsilon)
    slot = lax.broadcasted_iota(jnp.int32, (40, 256), 0)
    picker = jnp.concatenate(
        [jnp.where(slots_ref[r : r + 1, :] == slot, 1.0, 0.0) for r in range(16)], axis=0
    ).astype(jnp.bfloat16)
    for f in range(8):
        lanes = slice(f * 256, (f + 1) * 256)
        rows = (resid_ref[f].astype(jnp.float32) * level * gain_ref[:, lanes]).astype(jnp.bfloat16)
        mlp_ref[:, lanes] = rows
        picked = jnp.dot(picker, rows, preferred_element_type=jnp.float32)
        for r in range(16):
            out_ref[r, :, lanes] = picked[r * 40 : (r + 1) * 40].astype(jnp.bfloat16)


def dispatch(full_resid, gain, slots):
    return pl.pallas_call(
        dispatch_kernel,
        out_shape=(
            jax.ShapeDtypeStruct((256, D), jnp.bfloat16),
            jax.ShapeDtypeStruct((16, 40, D), jnp.bfloat16),
        ),
        name="dispatch",
    )(full_resid, gain, slots)


def expert_kernel(rows_ref, gate_up_ref, down_ref, out_ref):
    units = down_ref.shape[0]
    for part in range(2):
        rows = rows_ref[part * 320 : (part + 1) * 320, :]
        gate_up = jnp.dot(rows, gate_up_ref[...], preferred_element_type=jnp.float32)
        hidden = (jax.nn.silu(gate_up[:, :units]) * gate_up[:, units:]).astype(jnp.bfloat16)
        for f in range(8):
            result = jnp.dot(
                hidden, down_ref[:, f * 256 : (f + 1) * 256], preferred_element_type=jnp.float32
            )
            for r in range(8):
                out_ref[part * 8 + r, f] = result[r * 40 : (r + 1) * 40].astype(jnp.bfloat16)


def expert(rows, gate_up, down):
    return pl.pallas_call(
        expert_kernel,
        in_specs=in_vmem(3),
        out_shape=jax.ShapeDtypeStruct((16, 8, 40, 256), jnp.bfloat16),
        name="expert",
    )(rows, gate_up, down)


def place_rows_kernel(dest_ref, *refs):
    out_ref = refs[-1]
    total = jnp.zeros(out_ref.shape, jnp.float32)
    at = 0
    for ref in refs[:-1]:
        height = ref.shape[0]
        dest = dest_ref[:, at : at + height]
        rows = lax.broadcasted_iota(jnp.int32, (out_ref.shape[0], height), 0)
        mover = jnp.where(rows == dest, 1.0, 0.0).astype(jnp.bfloat16)
        total += jnp.dot(mover, ref[...], preferred_element_type=jnp.float32)
        at += height
    out_ref[...] = total.astype(out_ref.dtype)


def place_rows(dest, sources):
    return pl.pallas_call(
        place_rows_kernel,
        out_shape=jax.ShapeDtypeStruct((256, sources[0].shape[1]), sources[0].dtype),
        name="place_rows",
    )(dest, *sources)


def on_device(
    tokens,
    attn_gain,
    mlp_gain,
    trainer_qkv,
    trainer_out,
    router,
    shared_gate,
    shared_up,
    shared_down,
    expert_gate_up,
    expert_down,
    lengths,
    order,
    routes,
):
    tok_rows = tokens.shape[0]
    row_count, col_count = 16, 8
    zh_index = lax.axis_index("zh")
    y_index = lax.axis_index("y")
    k_index = lax.axis_index("k")
    row_index = lax.axis_index(ROW)
    col_index = lax.axis_index(COL)
    first = row_index * tok_rows
    local = jnp.arange(tok_rows, dtype=jnp.int32)

    seg_query, within_query, _ = prompt_tables(lengths, order, first + local)
    cosine, sine_part = rotary_tables(within_query, HEAD_DIM)
    start = (first + local - within_query)[:, None]

    heads = trainer_qkv.astype(jnp.bfloat16).reshape(16, 24, HEAD_DIM).transpose(1, 0, 2)
    groups = jnp.stack(
        [jnp.stack([heads[2 * g], heads[2 * g + 1], heads[16 + g // 2], heads[20 + g // 2]]) for g in range(8)]
    ).reshape(8, 64, HEAD_DIM)
    token_parts = tokens.reshape(tok_rows, 2, HEAD_DIM).transpose(1, 0, 2).reshape(1, 512, HEAD_DIM)
    out_parts = (
        trainer_out.astype(jnp.bfloat16).T.reshape(16, 8, 2, HEAD_DIM).transpose(1, 2, 0, 3)
    ).reshape(8, 32, HEAD_DIM)
    came = lax.all_to_all(
        jnp.concatenate(
            [groups, jnp.broadcast_to(token_parts, (8, 512, HEAD_DIM)), out_parts], axis=1
        ),
        COL, 0, 0, tiled=True,
    )
    qkv_heads = came[:, :64].reshape(8, 4, 16, HEAD_DIM).transpose(1, 0, 2, 3).reshape(4, 128, HEAD_DIM)
    qkv_block = qkv_heads.transpose(1, 0, 2).reshape(128, 512)
    out_block = came[:, 576:].reshape(8, 2, 16, HEAD_DIM).transpose(1, 3, 0, 2).reshape(256, 128)

    block = jnp.concatenate([qkv_heads.reshape(512, HEAD_DIM), out_block], axis=0)
    mine = lax.all_to_all(
        jnp.broadcast_to(block[None], (8, 768, HEAD_DIM)), ("zh", "y"), 0, 0, tiled=True
    )
    other = core_swap(mine)

    queries, kv_rows = projection(
        came, mine, other, attn_gain.reshape(16, HEAD_DIM), cosine, sine_part
    )
    cache_out = jnp.where(col_index % 2 == 0, kv_rows[:, :HEAD_DIM], kv_rows[:, HEAD_DIM:])

    tail = kv_rows[128:]
    head_sent = sum(lax.ppermute(tail, ROW, [(7, to)]) for to in (9, 11, 13, 15))
    head_sent, kv_copies = lax.optimization_barrier(
        (head_sent, jnp.broadcast_to(kv_rows[None], (4, 256, 256)))
    )
    kv_mine = lax.all_to_all(kv_copies, "y", 0, 0, tiled=True)
    kv_other = core_swap(kv_mine)
    kv_head = head_sent + core_swap(head_sent)
    terms = attention(queries, kv_mine, kv_other, kv_head, start, mine, other)
    got = lax.all_to_all(terms, COL, 0, 0, tiled=True)
    attn_part = jnp.sum(got.astype(jnp.float32), axis=0)
    resid = (tokens.astype(jnp.float32) + attn_part).astype(jnp.bfloat16)
    full_resid = col_gather(resid)

    n_experts = row_count * col_count // 2
    capacity = 40
    expert_ids = jnp.arange(n_experts, dtype=jnp.int32)
    member = jnp.any(routes[:, :, None] == expert_ids[None, None, :], axis=1)
    slot_of = jnp.where(member, jnp.cumsum(member.astype(jnp.int32), axis=0) - 1, -1)
    slots = lax.dynamic_index_in_dim(
        slot_of.reshape(tok_rows, row_count, col_count // 2), col_index // 2, 2, keepdims=False
    ).T
    mlp_in, outgoing = dispatch(full_resid, mlp_gain[None, :], slots)
    arrived = lax.all_to_all(outgoing, ROW, 0, 0, tiled=True)

    logits = jnp.dot(mlp_in, router, preferred_element_type=jnp.float32)
    router_probs = jax.nn.softmax(logits, axis=-1)
    picked_probs = jnp.where(member, router_probs, 0.0)
    route_weight = (
        picked_probs / jnp.sum(picked_probs, axis=-1, keepdims=True)
    ).astype(jnp.bfloat16)
    twice = jnp.repeat(slot_of, 2, axis=1)[:, :, None]
    combiner = jnp.where(
        twice == jnp.arange(capacity, dtype=jnp.int32),
        jnp.repeat(route_weight, 2, axis=1)[:, :, None],
        jnp.bfloat16(0),
    ).reshape(tok_rows, 2 * n_experts * capacity)
    shared_hidden = (
        jax.nn.silu(jnp.dot(mlp_in, shared_gate, preferred_element_type=jnp.float32))
        * jnp.dot(mlp_in, shared_up, preferred_element_type=jnp.float32)
    ).astype(jnp.bfloat16)
    shared_part = jnp.dot(shared_hidden, shared_down, preferred_element_type=jnp.float32).astype(
        jnp.bfloat16
    )
    pieces = []
    for step in range(col_count):
        piece = lax.dynamic_slice(shared_part, (0, (col_index ^ step) * 256), (tok_rows, 256))
        if step:
            piece = lax.ppermute(piece, COL, [(i, i ^ step) for i in range(col_count)])
        pieces.append(piece)
    arrived, combiner, pieces = lax.optimization_barrier((arrived, combiner, pieces))
    shared_sum = sum(piece.astype(jnp.float32) for piece in pieces)

    result = expert(arrived.reshape(row_count * capacity, D), expert_gate_up[0], expert_down[0])
    came_back = lax.all_to_all(
        result.reshape(2 * n_experts, capacity, 256), ROW + COL, 0, 0, tiled=True
    )
    routed_part = jnp.dot(
        combiner,
        came_back.reshape(2 * n_experts * capacity, 256),
        preferred_element_type=jnp.float32,
    )
    layer_out = (
        resid.astype(jnp.float32) + shared_sum + routed_part
    ).astype(jnp.bfloat16)

    received = []
    for step in range(4):
        pairs = [(s, 4 + (s + step) % 4) for s in range(4)]
        if step == 0:
            pairs += [(4 + s, s) for s in range(4)]
        received.append(lax.ppermute(layer_out, ("zh", "y"), pairs))
    late = lax.ppermute(
        layer_out[128:], ROW, [(7 + i, i) for i in range(0, 8, 2)] + [(15, 8)]
    )
    swapped = [core_swap(rows) for rows in received]
    span = jnp.arange(1024, dtype=jnp.int32)
    step_of = span // 256
    from_row = jnp.where(
        zh_index == 1,
        ((y_index - step_of) % 4) * 2,
        jnp.where(step_of == 0, 8 + y_index * 2, jnp.int32(1 << 12)),
    )
    late_from = jnp.where(
        k_index == 1, 1 << 12, jnp.where(zh_index == 0, row_index + 7, jnp.where(row_index == 8, 15, 1 << 12))
    )
    source_pos = jnp.concatenate(
        [
            (from_row + k_index) * 256 + span % 256,
            (from_row + 1 - k_index) * 256 + span % 256,
            late_from * 256 + 128 + jnp.arange(128, dtype=jnp.int32),
        ]
    )
    _, _, dest = prompt_tables(lengths, order, source_pos)
    dest = jnp.where(source_pos < row_count * tok_rows, dest, -1)
    hidden_states = place_rows((dest - first)[None, :], received + swapped + [late])
    return (hidden_states, cache_out, qkv_block, out_block)


def solution(mesh):
    fine = Mesh(mesh.devices.reshape(2, 4, 2, 2, 4), ROW + COL)
    in_specs = (
        P(ROW, COL),
        P(),
        P(),
        P(ROW + COL, None),
        P(None, ROW + COL),
        P(),
        P(None, COL),
        P(None, COL),
        P(COL, None),
        P(ROW + COL, None, None),
        P(ROW + COL, None, None),
        P(),
        P(),
        P(ROW, None),
    )
    out_specs = (P(ROW, COL), P(ROW, COL), P(ROW, COL), P(COL, ROW))
    return jax.shard_map(
        on_device, mesh=fine, in_specs=in_specs, out_specs=out_specs, check_vma=False
    )
```

```python
import jax
import jax.numpy as jnp
from jax import lax
from jax.experimental import pallas as pl
from jax.experimental.pallas import tpu as pltpu
from jax.sharding import Mesh
from jax.sharding import PartitionSpec as P

D = 2048
HEAD_DIM = 128
TOP = 6
FIRST_LONG = 1920

ROW = ("zh", "y", "k")
COL = ("zl", "x")

epsilon = 1e-06
rope_base = 600000.0
masked_score = -1e30


def prompt_tables(lengths, order, positions):
    prompt_ids = jnp.arange(lengths.shape[0], dtype=jnp.int32)
    picked = order[:, None] == prompt_ids[None, :]
    packed_len = jnp.sum(jnp.where(picked, lengths[None, :], 0), axis=1)
    packed_end = jnp.cumsum(packed_len)
    packed_start = packed_end - packed_len
    request_start = jnp.cumsum(lengths) - lengths
    segment = jnp.sum((positions[:, None] >= packed_end[None, :]).astype(jnp.int32), axis=1)
    onehot = segment[:, None] == prompt_ids[None, :]
    within = positions - jnp.sum(jnp.where(onehot, packed_start[None, :], 0), axis=1)
    request = jnp.sum(jnp.where(onehot, order[None, :], 0), axis=1)
    offset = jnp.sum(
        jnp.where(request[:, None] == prompt_ids[None, :], request_start[None, :], 0), axis=1
    )
    return (segment, within, within + offset)


def rms_scale(values, gain):
    wide = values.astype(jnp.float32)
    return wide * lax.rsqrt(jnp.mean(wide * wide, axis=-1, keepdims=True) + epsilon) * gain


def rotary_tables(within, size):
    half_dim = size // 2
    inverse = rope_base ** (-jnp.arange(half_dim, dtype=jnp.float32) * 2.0 / size)
    angles = within.astype(jnp.float32)[:, None] * inverse[None, :]
    cosine = jnp.cos(angles)
    sine_part = jnp.sin(angles)
    return (
        jnp.concatenate([cosine, cosine], axis=1),
        jnp.concatenate([-sine_part, sine_part], axis=1),
    )


def core_swap(block):
    return lax.ppermute(block, "k", [(0, 1), (1, 0)])


def col_gather(block):
    copies = jnp.broadcast_to(block[None], (8,) + block.shape)
    return lax.all_to_all(copies, COL, 0, 0, tiled=True)


def in_vmem(count):
    return [pl.BlockSpec(memory_space=pltpu.VMEM)] * count


def in_hbm(count):
    return [pl.BlockSpec(memory_space=pltpu.HBM)] * count


def projection_kernel(
    came_ref, mine_ref, other_ref, gain_ref, cos_ref, sin_ref, q_hbm, kv_ref, q_ref, sems
):
    core = lax.axis_index("k")
    squares = jnp.zeros((256, HEAD_DIM), jnp.float32)
    for member in range(8):
        for part in range(2):
            x = came_ref[member, 64 + part * 256 : 320 + part * 256, :].astype(jnp.float32)
            squares += x * x
    mean = jnp.sum(squares, axis=1, keepdims=True) * (1.0 / D)
    level = lax.rsqrt(mean + epsilon)
    total = jnp.zeros((256, 4 * HEAD_DIM), jnp.float32)
    for member in range(8):
        inputs, weights = [], []
        for part, ref in ((core, mine_ref), (1 - core, other_ref)):
            at = pl.multiple_of(64 + part * 256, 64)
            x = came_ref[member, pl.ds(at, 256), :].astype(jnp.float32)
            gain = gain_ref[pl.ds(2 * member + part, 1), :]
            inputs.append((x * level * gain).astype(jnp.bfloat16))
            weights.append(
                jnp.concatenate(
                    [ref[member, h * HEAD_DIM : (h + 1) * HEAD_DIM, :] for h in range(4)], axis=1
                )
            )
        total += jnp.dot(
            jnp.concatenate(inputs, axis=1),
            jnp.concatenate(weights, axis=0),
            preferred_element_type=jnp.float32,
        )
    cosine = cos_ref[...]
    sine_part = sin_ref[...]
    for h in range(4):
        part = total[:, h * HEAD_DIM : (h + 1) * HEAD_DIM]
        if h < 3:
            part = part * cosine + pltpu.roll(part, HEAD_DIM // 2, 1) * sine_part
        part = part.astype(jnp.bfloat16)
        if h < 2:
            q_ref[h] = part
        else:
            kv_ref[:, (h - 2) * HEAD_DIM : (h - 1) * HEAD_DIM] = part
        if h == 1:
            keep = pltpu.make_async_copy(q_ref, q_hbm, sems.at[0])
            keep.start()
    keep.wait()


def projection(came, mine, other, gain, cosine, sine_part):
    return pl.pallas_call(
        projection_kernel,
        in_specs=in_vmem(6),
        out_specs=in_hbm(1) + in_vmem(1),
        scratch_shapes=[
            pltpu.VMEM((2, 256, HEAD_DIM), jnp.bfloat16),
            pltpu.SemaphoreType.DMA((1,)),
        ],
        out_shape=(
            jax.ShapeDtypeStruct((2, 256, HEAD_DIM), jnp.bfloat16),
            jax.ShapeDtypeStruct((256, 2 * HEAD_DIM), jnp.bfloat16),
        ),
        compiler_params=pltpu.CompilerParams(vmem_limit_bytes=16 << 20),
        name="projection",
    )(came, mine, other, gain, cosine, sine_part)


def attention_kernel(
    q_hbm, mine_ref, other_ref, start_ref, out_mine_ref, out_other_ref, terms_ref, s_ref, q_ref, sems
):
    half, core = lax.axis_index("zh"), lax.axis_index("k")
    first = half * 2048 + lax.axis_index("y") * 512 + core * 256
    scale = HEAD_DIM ** (-0.5)
    query_pos = first + lax.broadcasted_iota(jnp.int32, (256, 1), 0)
    fetch = pltpu.make_async_copy(q_hbm, q_ref, sems.at[0])
    fetch.start()
    start = jnp.zeros((256, 1), jnp.int32)
    for slot in range(8):
        start = jnp.where(query_pos >= start_ref[slot], start_ref[slot], start)
    fetch.wait()
    blocks = []
    for y in range(4):
        blocks.append((mine_ref, y, half * 2048 + y * 512 + core * 256, 256))
        blocks.append((other_ref, y, half * 2048 + y * 512 + (1 - core) * 256, 256))
    blocks.append((None, 3, jnp.where(half == 1, FIRST_LONG, 1 << 20), 128))

    def piece(ref, index, lanes):
        if ref is None:
            return jnp.where(
                core == 1, mine_ref[index, 256:384, lanes], other_ref[index, 256:384, lanes]
            )
        return ref[index, :256, lanes]

    heads = []
    for h in range(2):
        query = q_ref[h]
        top = jnp.full((256, 128), masked_score, jnp.float32)
        at = 0
        for ref, index, pos, height in blocks:
            keys = piece(ref, index, slice(0, HEAD_DIM))
            scores = lax.dot_general(
                query, keys, (((1,), (1,)), ((), ())), preferred_element_type=jnp.float32
            ) * scale
            key_pos = pos + lax.broadcasted_iota(jnp.int32, (1, height), 1)
            allowed = (key_pos >= start) & (key_pos <= query_pos)
            scores = jnp.where(allowed, scores, masked_score)
            s_ref[:, at : at + height] = scores
            for lane in range(0, height, 128):
                top = jnp.maximum(top, scores[:, lane : lane + 128])
            at += height
        peak = jnp.max(top, axis=1, keepdims=True)
        sums = jnp.zeros((256, 128), jnp.float32)
        total = jnp.zeros((256, HEAD_DIM), jnp.float32)
        at = 0
        for ref, index, pos, height in blocks:
            numerators = jnp.exp(s_ref[:, at : at + height] - peak)
            for lane in range(0, height, 128):
                sums += numerators[:, lane : lane + 128]
            total += jnp.dot(
                numerators.astype(jnp.bfloat16),
                piece(ref, index, slice(HEAD_DIM, 2 * HEAD_DIM)),
                preferred_element_type=jnp.float32,
            )
            at += height
        heads.append((total / jnp.sum(sums, axis=1, keepdims=True)).astype(jnp.bfloat16))
    attended = jnp.concatenate(heads, axis=1)
    for f in range(8):
        mine = out_mine_ref[f, 512:768, :]
        other = out_other_ref[f, 512:768, :]
        low = jnp.where(core == 0, mine, other)
        high = jnp.where(core == 0, other, mine)
        terms_ref[f] = jnp.dot(
            attended, jnp.concatenate([low, high], axis=1), preferred_element_type=jnp.float32
        ).astype(jnp.bfloat16)


def attention(queries, mine, other, start, out_mine, out_other):
    return pl.pallas_call(
        attention_kernel,
        in_specs=in_hbm(1)
        + in_vmem(2)
        + [pl.BlockSpec(memory_space=pltpu.SMEM)]
        + in_vmem(2),
        out_shape=jax.ShapeDtypeStruct((8, 256, 256), jnp.bfloat16),
        scratch_shapes=[
            pltpu.VMEM((256, 2176), jnp.float32),
            pltpu.VMEM((2, 256, HEAD_DIM), jnp.bfloat16),
            pltpu.SemaphoreType.DMA((1,)),
        ],
        compiler_params=pltpu.CompilerParams(vmem_limit_bytes=24 << 20),
        name="attention",
    )(queries, mine, other, start, out_mine, out_other)


def dispatch_kernel(resid_ref, gain_ref, slots_ref, mlp_ref, out_ref):
    squares = jnp.zeros((256, 256), jnp.float32)
    for f in range(8):
        x = resid_ref[f].astype(jnp.float32)
        squares += x * x
    level = lax.rsqrt(jnp.sum(squares, axis=1, keepdims=True) * (1.0 / D) + epsilon)
    slot = lax.broadcasted_iota(jnp.int32, (40, 256), 0)
    picker = jnp.concatenate(
        [jnp.where(slots_ref[r : r + 1, :] == slot, 1.0, 0.0) for r in range(16)], axis=0
    ).astype(jnp.bfloat16)
    for f in range(8):
        lanes = slice(f * 256, (f + 1) * 256)
        rows = (resid_ref[f].astype(jnp.float32) * level * gain_ref[:, lanes]).astype(jnp.bfloat16)
        mlp_ref[:, lanes] = rows
        picked = jnp.dot(picker, rows, preferred_element_type=jnp.float32)
        for r in range(16):
            out_ref[r, :, lanes] = picked[r * 40 : (r + 1) * 40].astype(jnp.bfloat16)


def dispatch(full_resid, gain, slots):
    return pl.pallas_call(
        dispatch_kernel,
        out_shape=(
            jax.ShapeDtypeStruct((256, D), jnp.bfloat16),
            jax.ShapeDtypeStruct((16, 40, D), jnp.bfloat16),
        ),
        compiler_params=pltpu.CompilerParams(vmem_limit_bytes=16 << 20),
        name="dispatch",
    )(full_resid, gain, slots)


def shared_kernel(
    rows_hbm, gate_hbm, up_hbm, down_hbm, out_ref, rows_ref, gate_ref, up_ref, down_ref, sems
):
    pairs = ((rows_hbm, rows_ref), (gate_hbm, gate_ref), (up_hbm, up_ref), (down_hbm, down_ref))
    fetches = [
        pltpu.make_async_copy(source, target, sems.at[i]) for i, (source, target) in enumerate(pairs)
    ]
    for fetch in fetches:
        fetch.start()
    fetches[0].wait()
    fetches[1].wait()
    col = lax.axis_index("zl") * 4 + lax.axis_index("x")
    rows = rows_ref[...]
    across = (((1,), (1,)), ((), ()))
    gate = lax.dot_general(rows, gate_ref[...], across, preferred_element_type=jnp.float32)
    fetches[2].wait()
    up = lax.dot_general(rows, up_ref[...], across, preferred_element_type=jnp.float32)
    hidden = (jax.nn.silu(gate) * up).astype(jnp.bfloat16)
    fetches[3].wait()
    for f in range(8):
        out_ref[jnp.bitwise_xor(col, f)] = jnp.dot(
            hidden, down_ref[:, f * 256 : (f + 1) * 256], preferred_element_type=jnp.float32
        ).astype(jnp.bfloat16)


def shared(rows, gate, up, down):
    return pl.pallas_call(
        shared_kernel,
        in_specs=in_hbm(4),
        out_specs=in_vmem(1)[0],
        out_shape=jax.ShapeDtypeStruct((8, 256, 256), jnp.bfloat16),
        scratch_shapes=[
            pltpu.VMEM((256, D), jnp.bfloat16),
            pltpu.VMEM(gate.shape, jnp.bfloat16),
            pltpu.VMEM(up.shape, jnp.bfloat16),
            pltpu.VMEM(down.shape, jnp.bfloat16),
            pltpu.SemaphoreType.DMA((4,)),
        ],
        compiler_params=pltpu.CompilerParams(vmem_limit_bytes=60 << 20),
        name="shared",
    )(rows, gate, up, down)


def expert_kernel(
    rows_hbm, gate_up_hbm, down_hbm, out_hbm, rows_ref, gate_up_ref, down_ref, out_ref, fetch_sems, sems
):
    units = down_ref.shape[0]
    pairs = ((gate_up_hbm, gate_up_ref), (rows_hbm, rows_ref), (down_hbm, down_ref))
    fetches = [
        pltpu.make_async_copy(source, target, fetch_sems.at[i])
        for i, (source, target) in enumerate(pairs)
    ]
    for fetch in fetches:
        fetch.start()
    fetches[0].wait()
    fetches[1].wait()
    copies = []
    for part in range(2):
        rows = slice(part * 320, (part + 1) * 320)
        gate_up = jnp.dot(rows_ref[rows, :], gate_up_ref[...], preferred_element_type=jnp.float32)
        if part == 0:
            fetches[2].wait()
        hidden = (jax.nn.silu(gate_up[:, :units]) * gate_up[:, units:]).astype(jnp.bfloat16)
        for f in range(8):
            result = jnp.dot(
                hidden, down_ref[:, f * 256 : (f + 1) * 256], preferred_element_type=jnp.float32
            )
            for r in range(8):
                out_ref[part * 8 + r, f] = result[r * 40 : (r + 1) * 40].astype(jnp.bfloat16)
            there = (pl.ds(part * 8, 8), f)
            copies.append(
                pltpu.make_async_copy(out_ref.at[there], out_hbm.at[there], sems.at[part * 8 + f])
            )
            copies[-1].start()
    for copy in copies:
        copy.wait()


def expert(rows, gate_up, down):
    return pl.pallas_call(
        expert_kernel,
        in_specs=in_hbm(3),
        out_specs=in_hbm(1)[0],
        out_shape=jax.ShapeDtypeStruct((16, 8, 40, 256), jnp.bfloat16),
        scratch_shapes=[
            pltpu.VMEM(rows.shape, jnp.bfloat16),
            pltpu.VMEM(gate_up.shape, jnp.bfloat16),
            pltpu.VMEM(down.shape, jnp.bfloat16),
            pltpu.VMEM((16, 8, 40, 256), jnp.bfloat16),
            pltpu.SemaphoreType.DMA((3,)),
            pltpu.SemaphoreType.DMA((16,)),
        ],
        compiler_params=pltpu.CompilerParams(vmem_limit_bytes=60 << 20),
        name="expert",
    )(rows, gate_up, down)


def place_rows_kernel(dest_ref, *refs):
    out_ref = refs[-1]
    total = jnp.zeros(out_ref.shape, jnp.float32)
    at = 0
    for ref in refs[:-1]:
        height = ref.shape[0]
        dest = dest_ref[:, at : at + height]
        rows = lax.broadcasted_iota(jnp.int32, (out_ref.shape[0], height), 0)
        mover = jnp.where(rows == dest, 1.0, 0.0).astype(jnp.bfloat16)
        total += jnp.dot(mover, ref[...], preferred_element_type=jnp.float32)
        at += height
    out_ref[...] = total.astype(out_ref.dtype)


def place_rows(dest, sources):
    return pl.pallas_call(
        place_rows_kernel,
        out_shape=jax.ShapeDtypeStruct((256, sources[0].shape[1]), sources[0].dtype),
        compiler_params=pltpu.CompilerParams(vmem_limit_bytes=8 << 20),
        name="place_rows",
    )(dest, *sources)


def on_device(
    tokens,
    attn_gain,
    mlp_gain,
    trainer_qkv,
    trainer_out,
    router,
    shared_gate,
    shared_up,
    shared_down,
    expert_gate_up,
    expert_down,
    lengths,
    order,
    routes,
):
    tok_rows = tokens.shape[0]
    row_count, col_count = 16, 8
    zh_index = lax.axis_index("zh")
    y_index = lax.axis_index("y")
    k_index = lax.axis_index("k")
    row_index = lax.axis_index(ROW)
    col_index = lax.axis_index(COL)
    first = row_index * tok_rows
    local = jnp.arange(tok_rows, dtype=jnp.int32)

    seg_query, within_query, _ = prompt_tables(lengths, order, first + local)
    cosine, sine_part = rotary_tables(within_query, HEAD_DIM)
    packed = jnp.sum(
        jnp.where(order[:, None] == jnp.arange(8, dtype=jnp.int32)[None, :], lengths[None, :], 0), axis=1
    )
    start = jnp.cumsum(packed) - packed

    heads = trainer_qkv.astype(jnp.bfloat16).reshape(16, 24, HEAD_DIM).transpose(1, 0, 2)
    groups = jnp.stack(
        [jnp.stack([heads[2 * g], heads[2 * g + 1], heads[16 + g // 2], heads[20 + g // 2]]) for g in range(8)]
    ).reshape(8, 64, HEAD_DIM)
    token_parts = tokens.reshape(tok_rows, 2, HEAD_DIM).transpose(1, 0, 2).reshape(1, 512, HEAD_DIM)
    out_parts = (
        trainer_out.astype(jnp.bfloat16).T.reshape(16, 8, 2, HEAD_DIM).transpose(1, 2, 0, 3)
    ).reshape(8, 32, HEAD_DIM)
    came = lax.all_to_all(
        jnp.concatenate(
            [groups, jnp.broadcast_to(token_parts, (8, 512, HEAD_DIM)), out_parts], axis=1
        ),
        COL, 0, 0, tiled=True,
    )
    qkv_heads = came[:, :64].reshape(8, 4, 16, HEAD_DIM).transpose(1, 0, 2, 3).reshape(4, 128, HEAD_DIM)
    qkv_block = qkv_heads.transpose(1, 0, 2).reshape(128, 512)
    out_block = came[:, 576:].reshape(8, 2, 16, HEAD_DIM).transpose(1, 3, 0, 2).reshape(256, 128)

    block = jnp.concatenate([qkv_heads.reshape(512, HEAD_DIM), out_block], axis=0)
    mine = lax.all_to_all(
        jnp.broadcast_to(block[None], (8, 768, HEAD_DIM)), ("zh", "y"), 0, 0, tiled=True
    )
    other = core_swap(mine)

    queries, kv_rows = projection(
        came, mine, other, attn_gain.reshape(16, HEAD_DIM), cosine, sine_part
    )
    cache_out = jnp.where(col_index % 2 == 0, kv_rows[:, :HEAD_DIM], kv_rows[:, HEAD_DIM:])

    head_sent = lax.ppermute(kv_rows[128:], ROW, [(7, 15)])
    block = jnp.concatenate([kv_rows, head_sent], axis=0)
    kv_mine = lax.all_to_all(
        jnp.broadcast_to(block[None], (4, 384, 256)), "y", 0, 0, tiled=True
    )
    kv_other = core_swap(kv_mine)
    terms = attention(queries, kv_mine, kv_other, start, mine, other)
    got = lax.all_to_all(terms, COL, 0, 0, tiled=True)
    attn_part = jnp.sum(got.astype(jnp.float32), axis=0)
    resid = (tokens.astype(jnp.float32) + attn_part).astype(jnp.bfloat16)
    full_resid = col_gather(resid)

    n_experts = row_count * col_count // 2
    capacity = 40
    expert_ids = jnp.arange(n_experts, dtype=jnp.int32)
    member = jnp.any(routes[:, :, None] == expert_ids[None, None, :], axis=1)
    slot_of = jnp.where(member, jnp.cumsum(member.astype(jnp.int32), axis=0) - 1, -1)
    slots = lax.dynamic_index_in_dim(
        slot_of.reshape(tok_rows, row_count, col_count // 2), col_index // 2, 2, keepdims=False
    ).T
    mlp_in, outgoing = dispatch(full_resid, mlp_gain[None, :], slots)
    arrived = lax.all_to_all(outgoing, ROW, 0, 0, tiled=True)

    logits = jnp.dot(mlp_in, router, preferred_element_type=jnp.float32)
    router_probs = jax.nn.softmax(logits, axis=-1)
    picked_probs = jnp.where(member, router_probs, 0.0)
    route_weight = (
        picked_probs / jnp.sum(picked_probs, axis=-1, keepdims=True)
    ).astype(jnp.bfloat16)
    twice = jnp.repeat(slot_of, 2, axis=1)[:, :, None]
    combiner = jnp.where(
        twice == jnp.arange(capacity, dtype=jnp.int32),
        jnp.repeat(route_weight, 2, axis=1)[:, :, None],
        jnp.bfloat16(0),
    ).reshape(tok_rows, 2 * n_experts * capacity)
    shared_part = shared(mlp_in, shared_gate.T, shared_up.T, shared_down)
    pieces = []
    for step in range(col_count):
        piece = shared_part[step]
        if step:
            piece = lax.ppermute(piece, COL, [(i, i ^ step) for i in range(col_count)])
        pieces.append(piece)
    arrived, combiner, pieces, qkv_block, out_block, cache_out = lax.optimization_barrier(
        (arrived, combiner, pieces, qkv_block, out_block, cache_out)
    )
    shared_sum = sum(piece.astype(jnp.float32) for piece in pieces)

    result = expert(
        arrived.reshape(row_count * capacity, D), expert_gate_up[0], expert_down[0]
    )
    came_back = lax.all_to_all(
        result.reshape(2 * n_experts, capacity, 256), ROW + COL, 0, 0, tiled=True
    )
    routed_part = jnp.dot(
        combiner,
        came_back.reshape(2 * n_experts * capacity, 256),
        preferred_element_type=jnp.float32,
    )
    layer_out = (
        resid.astype(jnp.float32) + shared_sum + routed_part
    ).astype(jnp.bfloat16)

    received = []
    for step in range(4):
        pairs = [(s, 4 + (s + step) % 4) for s in range(4)]
        if step == 0:
            pairs += [(4 + s, s) for s in range(4)]
        received.append(lax.ppermute(layer_out, ("zh", "y"), pairs))
    late = lax.ppermute(
        layer_out[128:], ROW, [(7 + i, i) for i in range(0, 8, 2)] + [(15, 8)]
    )
    swapped = [core_swap(rows) for rows in received]
    span = jnp.arange(1024, dtype=jnp.int32)
    step_of = span // 256
    from_row = jnp.where(
        zh_index == 1,
        ((y_index - step_of) % 4) * 2,
        jnp.where(step_of == 0, 8 + y_index * 2, jnp.int32(1 << 12)),
    )
    late_from = jnp.where(
        k_index == 1, 1 << 12, jnp.where(zh_index == 0, row_index + 7, jnp.where(row_index == 8, 15, 1 << 12))
    )
    source_pos = jnp.concatenate(
        [
            (from_row + k_index) * 256 + span % 256,
            (from_row + 1 - k_index) * 256 + span % 256,
            late_from * 256 + 128 + jnp.arange(128, dtype=jnp.int32),
        ]
    )
    _, _, dest = prompt_tables(lengths, order, source_pos)
    dest = jnp.where(source_pos < row_count * tok_rows, dest, -1)
    hidden_states = place_rows((dest - first)[None, :], received + swapped + [late])
    return (hidden_states, cache_out, qkv_block, out_block)


def solution(mesh):
    fine = Mesh(mesh.devices.reshape(2, 4, 2, 2, 4), ROW + COL)
    in_specs = (
        P(ROW, COL),
        P(),
        P(),
        P(ROW + COL, None),
        P(None, ROW + COL),
        P(),
        P(None, COL),
        P(None, COL),
        P(COL, None),
        P(ROW + COL, None, None),
        P(ROW + COL, None, None),
        P(),
        P(),
        P(ROW, None),
    )
    out_specs = (P(ROW, COL), P(ROW, COL), P(ROW, COL), P(COL, ROW))
    return jax.shard_map(
        on_device, mesh=fine, in_specs=in_specs, out_specs=out_specs, check_vma=False
    )
```

```python
import jax
import jax.numpy as jnp
from jax import lax
from jax.experimental import pallas as pl
from jax.experimental.pallas import tpu as pltpu
from jax.sharding import Mesh
from jax.sharding import PartitionSpec as P

D = 2048
HEAD_DIM = 128
TOP = 6
FIRST_LONG = 1920

ROW = ("zh", "y", "k")
COL = ("zl", "x")
DIAGONALS = [
    [row * 8 + (low ^ (row // 8)) * 4 + x for row in range(16)] for low in range(2) for x in range(4)
]

epsilon = 1e-06
rope_base = 600000.0
masked_score = -1e30


def prompt_tables(lengths, order, positions):
    prompt_ids = jnp.arange(lengths.shape[0], dtype=jnp.int32)
    picked = order[:, None] == prompt_ids[None, :]
    packed_len = jnp.sum(jnp.where(picked, lengths[None, :], 0), axis=1)
    packed_end = jnp.cumsum(packed_len)
    packed_start = packed_end - packed_len
    request_start = jnp.cumsum(lengths) - lengths
    segment = jnp.sum((positions[:, None] >= packed_end[None, :]).astype(jnp.int32), axis=1)
    onehot = segment[:, None] == prompt_ids[None, :]
    within = positions - jnp.sum(jnp.where(onehot, packed_start[None, :], 0), axis=1)
    request = jnp.sum(jnp.where(onehot, order[None, :], 0), axis=1)
    offset = jnp.sum(
        jnp.where(request[:, None] == prompt_ids[None, :], request_start[None, :], 0), axis=1
    )
    return (segment, within, within + offset)


def rms_scale(values, gain):
    wide = values.astype(jnp.float32)
    return wide * lax.rsqrt(jnp.mean(wide * wide, axis=-1, keepdims=True) + epsilon) * gain


def rotary_tables(within, size):
    half_dim = size // 2
    inverse = rope_base ** (-jnp.arange(half_dim, dtype=jnp.float32) * 2.0 / size)
    angles = within.astype(jnp.float32)[:, None] * inverse[None, :]
    cosine = jnp.cos(angles)
    sine_part = jnp.sin(angles)
    return (
        jnp.concatenate([cosine, cosine], axis=1),
        jnp.concatenate([-sine_part, sine_part], axis=1),
    )


def core_swap(block):
    return lax.ppermute(block, "k", [(0, 1), (1, 0)])


def col_gather(block):
    copies = jnp.broadcast_to(block[None], (8,) + block.shape)
    return lax.all_to_all(copies, COL, 0, 0, tiled=True)


def in_vmem(count):
    return [pl.BlockSpec(memory_space=pltpu.VMEM)] * count


def in_hbm(count):
    return [pl.BlockSpec(memory_space=pltpu.HBM)] * count


def projection_kernel(
    came_ref, mine_ref, other_ref, gain_ref, cos_ref, sin_ref, q_hbm, kv_ref, q_ref, sems
):
    core = lax.axis_index("k")
    squares = jnp.zeros((256, HEAD_DIM), jnp.float32)
    for member in range(8):
        for part in range(2):
            x = came_ref[member, 64 + part * 256 : 320 + part * 256, :].astype(jnp.float32)
            squares += x * x
    mean = jnp.sum(squares, axis=1, keepdims=True) * (1.0 / D)
    level = lax.rsqrt(mean + epsilon)
    total = jnp.zeros((256, 4 * HEAD_DIM), jnp.float32)
    for member in range(8):
        inputs, weights = [], []
        for part, ref in ((core, mine_ref), (1 - core, other_ref)):
            at = pl.multiple_of(64 + part * 256, 64)
            x = came_ref[member, pl.ds(at, 256), :].astype(jnp.float32)
            gain = gain_ref[pl.ds(2 * member + part, 1), :]
            inputs.append((x * level * gain).astype(jnp.bfloat16))
            weights.append(
                jnp.concatenate(
                    [ref[member, h * HEAD_DIM : (h + 1) * HEAD_DIM, :] for h in range(4)], axis=1
                )
            )
        total += jnp.dot(
            jnp.concatenate(inputs, axis=1),
            jnp.concatenate(weights, axis=0),
            preferred_element_type=jnp.float32,
        )
    cosine = cos_ref[...]
    sine_part = sin_ref[...]
    for h in range(4):
        part = total[:, h * HEAD_DIM : (h + 1) * HEAD_DIM]
        if h < 3:
            part = part * cosine + pltpu.roll(part, HEAD_DIM // 2, 1) * sine_part
        part = part.astype(jnp.bfloat16)
        if h < 2:
            q_ref[h] = part
        else:
            kv_ref[:, (h - 2) * HEAD_DIM : (h - 1) * HEAD_DIM] = part
        if h == 1:
            keep = pltpu.make_async_copy(q_ref, q_hbm, sems.at[0])
            keep.start()
    keep.wait()


def projection(came, mine, other, gain, cosine, sine_part):
    return pl.pallas_call(
        projection_kernel,
        in_specs=in_vmem(6),
        out_specs=in_hbm(1) + in_vmem(1),
        scratch_shapes=[
            pltpu.VMEM((2, 256, HEAD_DIM), jnp.bfloat16),
            pltpu.SemaphoreType.DMA((1,)),
        ],
        out_shape=(
            jax.ShapeDtypeStruct((2, 256, HEAD_DIM), jnp.bfloat16),
            jax.ShapeDtypeStruct((256, 2 * HEAD_DIM), jnp.bfloat16),
        ),
        compiler_params=pltpu.CompilerParams(vmem_limit_bytes=16 << 20),
        name="projection",
    )(came, mine, other, gain, cosine, sine_part)


def attention_kernel(
    q_hbm, mine_ref, other_ref, start_ref, out_mine_ref, out_other_ref, terms_ref, s_ref, q_ref, sems
):
    half, core = lax.axis_index("zh"), lax.axis_index("k")
    first = half * 2048 + lax.axis_index("y") * 512 + core * 256
    scale = HEAD_DIM ** (-0.5)
    query_pos = first + lax.broadcasted_iota(jnp.int32, (256, 1), 0)
    fetch = pltpu.make_async_copy(q_hbm, q_ref, sems.at[0])
    fetch.start()
    start = jnp.zeros((256, 1), jnp.int32)
    for slot in range(8):
        start = jnp.where(query_pos >= start_ref[slot], start_ref[slot], start)
    fetch.wait()
    blocks = []
    for y in range(4):
        blocks.append((mine_ref, y, half * 2048 + y * 512 + core * 256, 256))
        blocks.append((other_ref, y, half * 2048 + y * 512 + (1 - core) * 256, 256))
    blocks.append((None, 3, jnp.where(half == 1, FIRST_LONG, 1 << 20), 128))

    def piece(ref, index, lanes):
        if ref is None:
            return jnp.where(
                core == 1, mine_ref[index, 256:384, lanes], other_ref[index, 256:384, lanes]
            )
        return ref[index, :256, lanes]

    heads = []
    for h in range(2):
        query = q_ref[h]
        top = jnp.full((256, 128), masked_score, jnp.float32)
        at = 0
        for ref, index, pos, height in blocks:
            keys = piece(ref, index, slice(0, HEAD_DIM))
            scores = lax.dot_general(
                query, keys, (((1,), (1,)), ((), ())), preferred_element_type=jnp.float32
            ) * scale
            key_pos = pos + lax.broadcasted_iota(jnp.int32, (1, height), 1)
            allowed = (key_pos >= start) & (key_pos <= query_pos)
            scores = jnp.where(allowed, scores, masked_score)
            s_ref[:, at : at + height] = scores
            for lane in range(0, height, 128):
                top = jnp.maximum(top, scores[:, lane : lane + 128])
            at += height
        peak = jnp.max(top, axis=1, keepdims=True)
        sums = jnp.zeros((256, 128), jnp.float32)
        total = jnp.zeros((256, HEAD_DIM), jnp.float32)
        at = 0
        for ref, index, pos, height in blocks:
            numerators = jnp.exp(s_ref[:, at : at + height] - peak)
            for lane in range(0, height, 128):
                sums += numerators[:, lane : lane + 128]
            total += jnp.dot(
                numerators.astype(jnp.bfloat16),
                piece(ref, index, slice(HEAD_DIM, 2 * HEAD_DIM)),
                preferred_element_type=jnp.float32,
            )
            at += height
        heads.append((total / jnp.sum(sums, axis=1, keepdims=True)).astype(jnp.bfloat16))
    attended = jnp.concatenate(heads, axis=1)
    for f in range(8):
        mine = out_mine_ref[f, 512:768, :]
        other = out_other_ref[f, 512:768, :]
        low = jnp.where(core == 0, mine, other)
        high = jnp.where(core == 0, other, mine)
        terms_ref[f] = jnp.dot(
            attended, jnp.concatenate([low, high], axis=1), preferred_element_type=jnp.float32
        ).astype(jnp.bfloat16)


def attention(queries, mine, other, start, out_mine, out_other):
    return pl.pallas_call(
        attention_kernel,
        in_specs=in_hbm(1)
        + in_vmem(2)
        + [pl.BlockSpec(memory_space=pltpu.SMEM)]
        + in_vmem(2),
        out_shape=jax.ShapeDtypeStruct((8, 256, 256), jnp.bfloat16),
        scratch_shapes=[
            pltpu.VMEM((256, 2176), jnp.float32),
            pltpu.VMEM((2, 256, HEAD_DIM), jnp.bfloat16),
            pltpu.SemaphoreType.DMA((1,)),
        ],
        compiler_params=pltpu.CompilerParams(vmem_limit_bytes=24 << 20),
        name="attention",
    )(queries, mine, other, start, out_mine, out_other)


def dispatch_kernel(resid_ref, gain_ref, slots_ref, mlp_ref, out_ref):
    squares = jnp.zeros((256, 256), jnp.float32)
    for f in range(8):
        x = resid_ref[f].astype(jnp.float32)
        squares += x * x
    level = lax.rsqrt(jnp.sum(squares, axis=1, keepdims=True) * (1.0 / D) + epsilon)
    slot = lax.broadcasted_iota(jnp.int32, (40, 256), 0)
    picker = jnp.concatenate(
        [jnp.where(slots_ref[r : r + 1, :] == slot, 1.0, 0.0) for r in range(16)], axis=0
    ).astype(jnp.bfloat16)
    for f in range(8):
        lanes = slice(f * 256, (f + 1) * 256)
        rows = (resid_ref[f].astype(jnp.float32) * level * gain_ref[:, lanes]).astype(jnp.bfloat16)
        mlp_ref[:, lanes] = rows
        picked = jnp.dot(picker, rows, preferred_element_type=jnp.float32)
        for r in range(16):
            out_ref[r, :, lanes] = picked[r * 40 : (r + 1) * 40].astype(jnp.bfloat16)


def dispatch(full_resid, gain, slots):
    return pl.pallas_call(
        dispatch_kernel,
        out_shape=(
            jax.ShapeDtypeStruct((256, D), jnp.bfloat16),
            jax.ShapeDtypeStruct((16, 40, D), jnp.bfloat16),
        ),
        compiler_params=pltpu.CompilerParams(vmem_limit_bytes=16 << 20),
        name="dispatch",
    )(full_resid, gain, slots)


def shared_kernel(
    rows_hbm, gate_hbm, up_hbm, down_hbm, out_ref, rows_ref, gate_ref, up_ref, down_ref, sems
):
    pairs = ((rows_hbm, rows_ref), (gate_hbm, gate_ref), (up_hbm, up_ref), (down_hbm, down_ref))
    fetches = [
        pltpu.make_async_copy(source, target, sems.at[i]) for i, (source, target) in enumerate(pairs)
    ]
    for fetch in fetches:
        fetch.start()
    fetches[0].wait()
    fetches[1].wait()
    col = lax.axis_index("zl") * 4 + lax.axis_index("x")
    rows = rows_ref[...]
    across = (((1,), (1,)), ((), ()))
    gate = lax.dot_general(rows, gate_ref[...], across, preferred_element_type=jnp.float32)
    fetches[2].wait()
    up = lax.dot_general(rows, up_ref[...], across, preferred_element_type=jnp.float32)
    hidden = (jax.nn.silu(gate) * up).astype(jnp.bfloat16)
    fetches[3].wait()
    for f in range(8):
        out_ref[jnp.bitwise_xor(col, f)] = jnp.dot(
            hidden, down_ref[:, f * 256 : (f + 1) * 256], preferred_element_type=jnp.float32
        ).astype(jnp.bfloat16)


def shared(rows, gate, up, down):
    return pl.pallas_call(
        shared_kernel,
        in_specs=in_hbm(4),
        out_specs=in_vmem(1)[0],
        out_shape=jax.ShapeDtypeStruct((8, 256, 256), jnp.bfloat16),
        scratch_shapes=[
            pltpu.VMEM((256, D), jnp.bfloat16),
            pltpu.VMEM(gate.shape, jnp.bfloat16),
            pltpu.VMEM(up.shape, jnp.bfloat16),
            pltpu.VMEM(down.shape, jnp.bfloat16),
            pltpu.SemaphoreType.DMA((4,)),
        ],
        compiler_params=pltpu.CompilerParams(vmem_limit_bytes=60 << 20),
        name="shared",
    )(rows, gate, up, down)


def expert_kernel(
    rows_hbm,
    gate_up_hbm,
    down_hbm,
    out_hbm,
    rows_ref,
    gate_up_ref,
    down_ref,
    out_ref,
    product_ref,
    fetch_sems,
    sems,
):
    units = down_ref.shape[0]
    widths = (0, 512, 1024, 2 * units)
    fetches = [
        pltpu.make_async_copy(rows_hbm.at[:320], rows_ref.at[:320], fetch_sems.at[3])
    ]
    for i in range(3):
        lanes = slice(widths[i], widths[i + 1])
        fetches.append(
            pltpu.make_async_copy(
                gate_up_hbm.at[:, lanes], gate_up_ref.at[:, lanes], fetch_sems.at[i]
            )
        )
    fetches.append(pltpu.make_async_copy(rows_hbm.at[320:], rows_ref.at[320:], fetch_sems.at[4]))
    fetches.append(pltpu.make_async_copy(down_hbm, down_ref, fetch_sems.at[5]))
    for fetch in fetches:
        fetch.start()
    fetches[0].wait()
    copies = []
    for part in range(2):
        rows = slice(part * 320, (part + 1) * 320)
        if part == 0:
            for i in range(3):
                lanes = slice(widths[i], widths[i + 1])
                fetches[1 + i].wait()
                product_ref[:, lanes] = jnp.dot(
                    rows_ref[rows, :], gate_up_ref[:, lanes], preferred_element_type=jnp.float32
                )
            gate_up = product_ref[...]
            fetches[4].wait()
            fetches[5].wait()
        else:
            gate_up = jnp.dot(
                rows_ref[rows, :], gate_up_ref[...], preferred_element_type=jnp.float32
            )
        hidden = (jax.nn.silu(gate_up[:, :units]) * gate_up[:, units:]).astype(jnp.bfloat16)
        for f in range(8):
            result = jnp.dot(
                hidden, down_ref[:, f * 256 : (f + 1) * 256], preferred_element_type=jnp.float32
            )
            for r in range(8):
                out_ref[part * 8 + r, f] = result[r * 40 : (r + 1) * 40].astype(jnp.bfloat16)
            there = (pl.ds(part * 8, 8), f)
            copies.append(
                pltpu.make_async_copy(out_ref.at[there], out_hbm.at[there], sems.at[part * 8 + f])
            )
            copies[-1].start()
    for copy in copies:
        copy.wait()


def expert(rows, gate_up, down):
    return pl.pallas_call(
        expert_kernel,
        in_specs=in_hbm(3),
        out_specs=in_hbm(1)[0],
        out_shape=jax.ShapeDtypeStruct((16, 8, 40, 256), jnp.bfloat16),
        scratch_shapes=[
            pltpu.VMEM(rows.shape, jnp.bfloat16),
            pltpu.VMEM(gate_up.shape, jnp.bfloat16),
            pltpu.VMEM(down.shape, jnp.bfloat16),
            pltpu.VMEM((16, 8, 40, 256), jnp.bfloat16),
            pltpu.VMEM((320, gate_up.shape[1]), jnp.float32),
            pltpu.SemaphoreType.DMA((6,)),
            pltpu.SemaphoreType.DMA((16,)),
        ],
        compiler_params=pltpu.CompilerParams(vmem_limit_bytes=60 << 20),
        name="expert",
    )(rows, gate_up, down)


def place_rows_kernel(dest_ref, *refs):
    out_ref = refs[-1]
    total = jnp.zeros(out_ref.shape, jnp.float32)
    at = 0
    for ref in refs[:-1]:
        height = ref.shape[0]
        dest = dest_ref[:, at : at + height]
        rows = lax.broadcasted_iota(jnp.int32, (out_ref.shape[0], height), 0)
        mover = jnp.where(rows == dest, 1.0, 0.0).astype(jnp.bfloat16)
        total += jnp.dot(mover, ref[...], preferred_element_type=jnp.float32)
        at += height
    out_ref[...] = total.astype(out_ref.dtype)


def place_rows(dest, sources):
    return pl.pallas_call(
        place_rows_kernel,
        out_shape=jax.ShapeDtypeStruct((256, sources[0].shape[1]), sources[0].dtype),
        compiler_params=pltpu.CompilerParams(vmem_limit_bytes=8 << 20),
        name="place_rows",
    )(dest, *sources)


def on_device(
    tokens,
    attn_gain,
    mlp_gain,
    trainer_qkv,
    trainer_out,
    router,
    shared_gate,
    shared_up,
    shared_down,
    expert_gate_up,
    expert_down,
    lengths,
    order,
    routes,
):
    tok_rows = tokens.shape[0]
    row_count, col_count = 16, 8
    zh_index = lax.axis_index("zh")
    y_index = lax.axis_index("y")
    k_index = lax.axis_index("k")
    row_index = lax.axis_index(ROW)
    col_index = lax.axis_index(COL)
    first = row_index * tok_rows
    local = jnp.arange(tok_rows, dtype=jnp.int32)

    seg_query, within_query, _ = prompt_tables(lengths, order, first + local)
    cosine, sine_part = rotary_tables(within_query, HEAD_DIM)
    packed = jnp.sum(
        jnp.where(order[:, None] == jnp.arange(8, dtype=jnp.int32)[None, :], lengths[None, :], 0), axis=1
    )
    start = jnp.cumsum(packed) - packed

    heads = trainer_qkv.astype(jnp.bfloat16).reshape(16, 24, HEAD_DIM).transpose(1, 0, 2)
    groups = jnp.stack(
        [jnp.stack([heads[2 * g], heads[2 * g + 1], heads[16 + g // 2], heads[20 + g // 2]]) for g in range(8)]
    ).reshape(8, 64, HEAD_DIM)
    token_parts = tokens.reshape(tok_rows, 2, HEAD_DIM).transpose(1, 0, 2).reshape(1, 512, HEAD_DIM)
    out_parts = (
        trainer_out.astype(jnp.bfloat16).T.reshape(16, 8, 2, HEAD_DIM).transpose(1, 2, 0, 3)
    ).reshape(8, 32, HEAD_DIM)
    came = lax.all_to_all(
        jnp.concatenate(
            [groups, jnp.broadcast_to(token_parts, (8, 512, HEAD_DIM)), out_parts], axis=1
        ),
        COL, 0, 0, tiled=True,
    )
    qkv_heads = came[:, :64].reshape(8, 4, 16, HEAD_DIM).transpose(1, 0, 2, 3).reshape(4, 128, HEAD_DIM)
    qkv_block = qkv_heads.transpose(1, 0, 2).reshape(128, 512)
    out_block = came[:, 576:].reshape(8, 2, 16, HEAD_DIM).transpose(1, 3, 0, 2).reshape(256, 128)

    block = jnp.concatenate([qkv_heads.reshape(512, HEAD_DIM), out_block], axis=0)
    mine = lax.all_to_all(
        jnp.broadcast_to(block[None], (8, 768, HEAD_DIM)), ("zh", "y"), 0, 0, tiled=True
    )
    other = core_swap(mine)

    queries, kv_rows = projection(
        came, mine, other, attn_gain.reshape(16, HEAD_DIM), cosine, sine_part
    )
    cache_out = jnp.where(col_index % 2 == 0, kv_rows[:, :HEAD_DIM], kv_rows[:, HEAD_DIM:])

    head_sent = lax.ppermute(kv_rows[128:], ROW, [(7, 15)])
    block = jnp.concatenate([kv_rows, head_sent], axis=0)
    kv_mine = lax.all_to_all(
        jnp.broadcast_to(block[None], (4, 384, 256)), "y", 0, 0, tiled=True
    )
    kv_other = core_swap(kv_mine)
    terms = attention(queries, kv_mine, kv_other, start, mine, other)
    got = lax.all_to_all(terms, COL, 0, 0, tiled=True)
    attn_part = jnp.sum(got.astype(jnp.float32), axis=0)
    resid = (tokens.astype(jnp.float32) + attn_part).astype(jnp.bfloat16)
    full_resid = col_gather(resid)

    n_experts = row_count * col_count // 2
    capacity = 40
    expert_ids = jnp.arange(n_experts, dtype=jnp.int32)
    member = jnp.any(routes[:, :, None] == expert_ids[None, None, :], axis=1)
    slot_of = jnp.where(member, jnp.cumsum(member.astype(jnp.int32), axis=0) - 1, -1)
    by_quarter = slot_of.reshape(tok_rows, row_count, col_count // 2)
    quarter = col_index // 2
    straight = lax.dynamic_index_in_dim(by_quarter, quarter, 2, keepdims=False)
    crossed = lax.dynamic_index_in_dim(by_quarter, quarter ^ 2, 2, keepdims=False)
    same_half = (jnp.arange(row_count) // 8 == zh_index)[None, :]
    slots = jnp.where(same_half, straight, crossed).T
    mlp_in, outgoing = dispatch(full_resid, mlp_gain[None, :], slots)
    arrived = lax.all_to_all(
        outgoing, ROW + COL, 0, 0, axis_index_groups=DIAGONALS, tiled=True
    )

    logits = jnp.dot(mlp_in, router, preferred_element_type=jnp.float32)
    router_probs = jax.nn.softmax(logits, axis=-1)
    picked_probs = jnp.where(member, router_probs, 0.0)
    route_weight = (
        picked_probs / jnp.sum(picked_probs, axis=-1, keepdims=True)
    ).astype(jnp.bfloat16)
    twice = jnp.repeat(slot_of, 2, axis=1)[:, :, None]
    combiner = jnp.where(
        twice == jnp.arange(capacity, dtype=jnp.int32),
        jnp.repeat(route_weight, 2, axis=1)[:, :, None],
        jnp.bfloat16(0),
    ).reshape(tok_rows, 2 * n_experts * capacity)
    shared_part = shared(mlp_in, shared_gate.T, shared_up.T, shared_down)
    pieces = []
    for step in range(col_count):
        piece = shared_part[step]
        if step:
            piece = lax.ppermute(piece, COL, [(i, i ^ step) for i in range(col_count)])
        pieces.append(piece)
    arrived, combiner, pieces, qkv_block, out_block, cache_out = lax.optimization_barrier(
        (arrived, combiner, pieces, qkv_block, out_block, cache_out)
    )
    shared_sum = sum(piece.astype(jnp.float32) for piece in pieces)

    result = expert(
        arrived.reshape(row_count * capacity, D), expert_gate_up[0], expert_down[0]
    )
    came_back = lax.all_to_all(
        result.reshape(2 * n_experts, capacity, 256), ROW + COL, 0, 0, tiled=True
    )
    routed_part = jnp.dot(
        combiner,
        came_back.reshape(2 * n_experts * capacity, 256),
        preferred_element_type=jnp.float32,
    )
    layer_out = (
        resid.astype(jnp.float32) + shared_sum + routed_part
    ).astype(jnp.bfloat16)

    received = []
    for step in range(4):
        pairs = [(s, 4 + (s + step) % 4) for s in range(4)]
        if step == 0:
            pairs += [(4 + s, s) for s in range(4)]
        received.append(lax.ppermute(layer_out, ("zh", "y"), pairs))
    late = lax.ppermute(
        layer_out[128:], ROW, [(7 + i, i) for i in range(0, 8, 2)] + [(15, 8)]
    )
    swapped = [core_swap(rows) for rows in received]
    span = jnp.arange(1024, dtype=jnp.int32)
    step_of = span // 256
    from_row = jnp.where(
        zh_index == 1,
        ((y_index - step_of) % 4) * 2,
        jnp.where(step_of == 0, 8 + y_index * 2, jnp.int32(1 << 12)),
    )
    late_from = jnp.where(
        k_index == 1, 1 << 12, jnp.where(zh_index == 0, row_index + 7, jnp.where(row_index == 8, 15, 1 << 12))
    )
    source_pos = jnp.concatenate(
        [
            (from_row + k_index) * 256 + span % 256,
            (from_row + 1 - k_index) * 256 + span % 256,
            late_from * 256 + 128 + jnp.arange(128, dtype=jnp.int32),
        ]
    )
    _, _, dest = prompt_tables(lengths, order, source_pos)
    dest = jnp.where(source_pos < row_count * tok_rows, dest, -1)
    hidden_states = place_rows((dest - first)[None, :], received + swapped + [late])
    return (hidden_states, cache_out, qkv_block, out_block)


def solution(mesh):
    fine = Mesh(mesh.devices.reshape(2, 4, 2, 2, 4), ROW + COL)
    in_specs = (
        P(ROW, COL),
        P(),
        P(),
        P(ROW + COL, None),
        P(None, ROW + COL),
        P(),
        P(None, COL),
        P(None, COL),
        P(COL, None),
        P(ROW + COL, None, None),
        P(ROW + COL, None, None),
        P(),
        P(),
        P(ROW, None),
    )
    out_specs = (P(ROW, COL), P(ROW, COL), P(ROW, COL), P(COL, ROW))
    return jax.shard_map(
        on_device, mesh=fine, in_specs=in_specs, out_specs=out_specs, check_vma=False
    )
```

```python
import jax
import jax.numpy as jnp
from jax import lax
from jax.experimental import pallas as pl
from jax.experimental.pallas import tpu as pltpu
from jax.sharding import Mesh
from jax.sharding import PartitionSpec as P

D = 2048
HEAD_DIM = 128
TOP = 6
FIRST_LONG = 1920

ROW = ("zh", "y", "k")
COL = ("zl", "x")
DIAGONALS = [
    [row * 8 + (low ^ (row // 8)) * 4 + x for row in range(16)] for low in range(2) for x in range(4)
]

epsilon = 1e-06
rope_base = 600000.0
masked_score = -1e30


def prompt_tables(lengths, order, positions):
    prompt_ids = jnp.arange(lengths.shape[0], dtype=jnp.int32)
    picked = order[:, None] == prompt_ids[None, :]
    packed_len = jnp.sum(jnp.where(picked, lengths[None, :], 0), axis=1)
    packed_end = jnp.cumsum(packed_len)
    packed_start = packed_end - packed_len
    request_start = jnp.cumsum(lengths) - lengths
    segment = jnp.sum((positions[:, None] >= packed_end[None, :]).astype(jnp.int32), axis=1)
    onehot = segment[:, None] == prompt_ids[None, :]
    within = positions - jnp.sum(jnp.where(onehot, packed_start[None, :], 0), axis=1)
    request = jnp.sum(jnp.where(onehot, order[None, :], 0), axis=1)
    offset = jnp.sum(
        jnp.where(request[:, None] == prompt_ids[None, :], request_start[None, :], 0), axis=1
    )
    return (segment, within, within + offset)


def rms_scale(values, gain):
    wide = values.astype(jnp.float32)
    return wide * lax.rsqrt(jnp.mean(wide * wide, axis=-1, keepdims=True) + epsilon) * gain


def rotary_tables(within, size):
    half_dim = size // 2
    inverse = rope_base ** (-jnp.arange(half_dim, dtype=jnp.float32) * 2.0 / size)
    angles = within.astype(jnp.float32)[:, None] * inverse[None, :]
    cosine = jnp.cos(angles)
    sine_part = jnp.sin(angles)
    return (
        jnp.concatenate([cosine, cosine], axis=1),
        jnp.concatenate([-sine_part, sine_part], axis=1),
    )


def core_swap(block):
    return lax.ppermute(block, "k", [(0, 1), (1, 0)])


def col_gather(block):
    copies = jnp.broadcast_to(block[None], (8,) + block.shape)
    return lax.all_to_all(copies, COL, 0, 0, tiled=True)


def in_vmem(count):
    return [pl.BlockSpec(memory_space=pltpu.VMEM)] * count


def in_hbm(count):
    return [pl.BlockSpec(memory_space=pltpu.HBM)] * count


def projection_kernel(
    came_ref, mine_ref, other_ref, gain_ref, cos_ref, sin_ref, q_hbm, kv_ref, q_ref, sems
):
    core = lax.axis_index("k")
    squares = jnp.zeros((256, HEAD_DIM), jnp.float32)
    for member in range(8):
        for part in range(2):
            x = came_ref[member, 64 + part * 256 : 320 + part * 256, :].astype(jnp.float32)
            squares += x * x
    mean = jnp.sum(squares, axis=1, keepdims=True) * (1.0 / D)
    level = lax.rsqrt(mean + epsilon)
    total = jnp.zeros((256, 4 * HEAD_DIM), jnp.float32)
    for member in range(8):
        inputs, weights = [], []
        for part, ref in ((core, mine_ref), (1 - core, other_ref)):
            at = pl.multiple_of(64 + part * 256, 64)
            x = came_ref[member, pl.ds(at, 256), :].astype(jnp.float32)
            gain = gain_ref[pl.ds(2 * member + part, 1), :]
            inputs.append((x * level * gain).astype(jnp.bfloat16))
            weights.append(
                jnp.concatenate(
                    [ref[member, h * HEAD_DIM : (h + 1) * HEAD_DIM, :] for h in range(4)], axis=1
                )
            )
        total += jnp.dot(
            jnp.concatenate(inputs, axis=1),
            jnp.concatenate(weights, axis=0),
            preferred_element_type=jnp.float32,
        )
    cosine = cos_ref[...]
    sine_part = sin_ref[...]
    for h in range(4):
        part = total[:, h * HEAD_DIM : (h + 1) * HEAD_DIM]
        if h < 3:
            part = part * cosine + pltpu.roll(part, HEAD_DIM // 2, 1) * sine_part
        part = part.astype(jnp.bfloat16)
        if h < 2:
            q_ref[h] = part
        else:
            kv_ref[:, (h - 2) * HEAD_DIM : (h - 1) * HEAD_DIM] = part
        if h == 1:
            keep = pltpu.make_async_copy(q_ref, q_hbm, sems.at[0])
            keep.start()
    keep.wait()


def projection(came, mine, other, gain, cosine, sine_part):
    return pl.pallas_call(
        projection_kernel,
        in_specs=in_vmem(6),
        out_specs=in_hbm(1) + in_vmem(1),
        scratch_shapes=[
            pltpu.VMEM((2, 256, HEAD_DIM), jnp.bfloat16),
            pltpu.SemaphoreType.DMA((1,)),
        ],
        out_shape=(
            jax.ShapeDtypeStruct((2, 256, HEAD_DIM), jnp.bfloat16),
            jax.ShapeDtypeStruct((256, 2 * HEAD_DIM), jnp.bfloat16),
        ),
        compiler_params=pltpu.CompilerParams(vmem_limit_bytes=16 << 20),
        name="projection",
    )(came, mine, other, gain, cosine, sine_part)


def attention_kernel(
    q_hbm, mine_ref, other_ref, start_ref, out_mine_ref, out_other_ref, terms_ref, qkv_ref, out_ref, s_ref, q_ref, sems
):
    half, core = lax.axis_index("zh"), lax.axis_index("k")
    first = half * 2048 + lax.axis_index("y") * 512 + core * 256
    scale = HEAD_DIM ** (-0.5)
    query_pos = first + lax.broadcasted_iota(jnp.int32, (256, 1), 0)
    fetch = pltpu.make_async_copy(q_hbm, q_ref, sems.at[0])
    fetch.start()
    start = jnp.zeros((256, 1), jnp.int32)
    for slot in range(8):
        start = jnp.where(query_pos >= start_ref[slot], start_ref[slot], start)
    fetch.wait()
    blocks = []
    for y in range(4):
        blocks.append((mine_ref, y, half * 2048 + y * 512 + core * 256, 256))
        blocks.append((other_ref, y, half * 2048 + y * 512 + (1 - core) * 256, 256))
    blocks.append((None, 3, jnp.where(half == 1, FIRST_LONG, 1 << 20), 128))

    def piece(ref, index, lanes):
        if ref is None:
            return jnp.where(
                core == 1, mine_ref[index, 256:384, lanes], other_ref[index, 256:384, lanes]
            )
        return ref[index, :256, lanes]

    heads = []
    for h in range(2):
        query = q_ref[h]
        top = jnp.full((256, 128), masked_score, jnp.float32)
        at = 0
        for ref, index, pos, height in blocks:
            keys = piece(ref, index, slice(0, HEAD_DIM))
            scores = lax.dot_general(
                query, keys, (((1,), (1,)), ((), ())), preferred_element_type=jnp.float32
            ) * scale
            key_pos = pos + lax.broadcasted_iota(jnp.int32, (1, height), 1)
            allowed = (key_pos >= start) & (key_pos <= query_pos)
            scores = jnp.where(allowed, scores, masked_score)
            s_ref[:, at : at + height] = scores
            for lane in range(0, height, 128):
                top = jnp.maximum(top, scores[:, lane : lane + 128])
            at += height
        peak = jnp.max(top, axis=1, keepdims=True)
        sums = jnp.zeros((256, 128), jnp.float32)
        total = jnp.zeros((256, HEAD_DIM), jnp.float32)
        at = 0
        for ref, index, pos, height in blocks:
            numerators = jnp.exp(s_ref[:, at : at + height] - peak)
            for lane in range(0, height, 128):
                sums += numerators[:, lane : lane + 128]
            total += jnp.dot(
                numerators.astype(jnp.bfloat16),
                piece(ref, index, slice(HEAD_DIM, 2 * HEAD_DIM)),
                preferred_element_type=jnp.float32,
            )
            at += height
        heads.append((total / jnp.sum(sums, axis=1, keepdims=True)).astype(jnp.bfloat16))
    attended = jnp.concatenate(heads, axis=1)
    own = half * 4 + lax.axis_index("y")
    for h in range(4):
        lanes = slice(h * HEAD_DIM, (h + 1) * HEAD_DIM)
        qkv_ref[:, lanes] = out_mine_ref[own, lanes, :]
    out_ref[...] = out_mine_ref[own, 512:768, :]
    for f in range(8):
        mine = out_mine_ref[f, 512:768, :]
        other = out_other_ref[f, 512:768, :]
        low = jnp.where(core == 0, mine, other)
        high = jnp.where(core == 0, other, mine)
        terms_ref[f] = jnp.dot(
            attended, jnp.concatenate([low, high], axis=1), preferred_element_type=jnp.float32
        ).astype(jnp.bfloat16)


def attention(queries, mine, other, start, out_mine, out_other):
    return pl.pallas_call(
        attention_kernel,
        in_specs=in_hbm(1)
        + in_vmem(2)
        + [pl.BlockSpec(memory_space=pltpu.SMEM)]
        + in_vmem(2),
        out_shape=(
            jax.ShapeDtypeStruct((8, 256, 256), jnp.bfloat16),
            jax.ShapeDtypeStruct((128, 512), jnp.bfloat16),
            jax.ShapeDtypeStruct((256, 128), jnp.bfloat16),
        ),
        scratch_shapes=[
            pltpu.VMEM((256, 2176), jnp.float32),
            pltpu.VMEM((2, 256, HEAD_DIM), jnp.bfloat16),
            pltpu.SemaphoreType.DMA((1,)),
        ],
        compiler_params=pltpu.CompilerParams(vmem_limit_bytes=24 << 20),
        name="attention",
    )(queries, mine, other, start, out_mine, out_other)


def dispatch_kernel(resid_ref, gain_ref, slots_ref, out_ref):
    squares = jnp.zeros((256, 256), jnp.float32)
    for f in range(8):
        x = resid_ref[f].astype(jnp.float32)
        squares += x * x
    level = lax.rsqrt(jnp.sum(squares, axis=1, keepdims=True) * (1.0 / D) + epsilon)
    slot = lax.broadcasted_iota(jnp.int32, (40, 256), 0)
    picker = jnp.concatenate(
        [jnp.where(slots_ref[r : r + 1, :] == slot, 1.0, 0.0) for r in range(16)], axis=0
    ).astype(jnp.bfloat16)
    for f in range(8):
        lanes = slice(f * 256, (f + 1) * 256)
        rows = (resid_ref[f].astype(jnp.float32) * level * gain_ref[:, lanes]).astype(jnp.bfloat16)
        picked = jnp.dot(picker, rows, preferred_element_type=jnp.float32)
        for r in range(16):
            out_ref[r, :, lanes] = picked[r * 40 : (r + 1) * 40].astype(jnp.bfloat16)


def dispatch(full_resid, gain, slots):
    return pl.pallas_call(
        dispatch_kernel,
        out_shape=jax.ShapeDtypeStruct((16, 40, D), jnp.bfloat16),
        compiler_params=pltpu.CompilerParams(vmem_limit_bytes=16 << 20),
        name="dispatch",
    )(full_resid, gain, slots)


def shared_kernel(
    resid_hbm,
    gain_ref,
    router_ref,
    gate_hbm,
    up_hbm,
    down_hbm,
    out_ref,
    logits_ref,
    resid_ref,
    rows_ref,
    gate_ref,
    up_ref,
    down_ref,
    sems,
):
    pairs = ((resid_hbm, resid_ref), (gate_hbm, gate_ref), (up_hbm, up_ref), (down_hbm, down_ref))
    fetches = [
        pltpu.make_async_copy(source, target, sems.at[i]) for i, (source, target) in enumerate(pairs)
    ]
    for fetch in fetches:
        fetch.start()
    col = lax.axis_index("zl") * 4 + lax.axis_index("x")
    fetches[0].wait()
    squares = jnp.zeros((256, 256), jnp.float32)
    for f in range(8):
        x = resid_ref[f].astype(jnp.float32)
        squares += x * x
    level = lax.rsqrt(jnp.sum(squares, axis=1, keepdims=True) * (1.0 / D) + epsilon)
    for f in range(8):
        lanes = slice(f * 256, (f + 1) * 256)
        rows_ref[:, lanes] = (
            resid_ref[f].astype(jnp.float32) * level * gain_ref[:, lanes]
        ).astype(jnp.bfloat16)
    rows = rows_ref[...]
    fetches[1].wait()
    across = (((1,), (1,)), ((), ()))
    logits_ref[...] = lax.dot_general(
        rows, router_ref[...], across, preferred_element_type=jnp.float32
    )
    gate = lax.dot_general(rows, gate_ref[...], across, preferred_element_type=jnp.float32)
    fetches[2].wait()
    up = lax.dot_general(rows, up_ref[...], across, preferred_element_type=jnp.float32)
    hidden = (jax.nn.silu(gate) * up).astype(jnp.bfloat16)
    fetches[3].wait()
    for f in range(8):
        out_ref[jnp.bitwise_xor(col, f)] = jnp.dot(
            hidden, down_ref[:, f * 256 : (f + 1) * 256], preferred_element_type=jnp.float32
        ).astype(jnp.bfloat16)


def shared(resid, gain, router, gate, up, down):
    return pl.pallas_call(
        shared_kernel,
        in_specs=in_hbm(1) + in_vmem(2) + in_hbm(3),
        out_specs=in_vmem(2),
        out_shape=(
            jax.ShapeDtypeStruct((8, 256, 256), jnp.bfloat16),
            jax.ShapeDtypeStruct((256, 64), jnp.float32),
        ),
        scratch_shapes=[
            pltpu.VMEM((8, 256, 256), jnp.bfloat16),
            pltpu.VMEM((256, D), jnp.bfloat16),
            pltpu.VMEM(gate.shape, jnp.bfloat16),
            pltpu.VMEM(up.shape, jnp.bfloat16),
            pltpu.VMEM(down.shape, jnp.bfloat16),
            pltpu.SemaphoreType.DMA((4,)),
        ],
        compiler_params=pltpu.CompilerParams(vmem_limit_bytes=60 << 20),
        name="shared",
    )(resid, gain, router, gate, up, down)


def expert_kernel(
    rows_hbm,
    gate_up_hbm,
    down_hbm,
    out_hbm,
    rows_ref,
    gate_up_ref,
    down_ref,
    out_ref,
    product_ref,
    fetch_sems,
    sems,
):
    units = down_ref.shape[0]
    widths = (0, 512, 1024, 2 * units)
    fetches = [
        pltpu.make_async_copy(rows_hbm.at[:320], rows_ref.at[:320], fetch_sems.at[3])
    ]
    for i in range(3):
        lanes = slice(widths[i], widths[i + 1])
        fetches.append(
            pltpu.make_async_copy(
                gate_up_hbm.at[:, lanes], gate_up_ref.at[:, lanes], fetch_sems.at[i]
            )
        )
    fetches.append(pltpu.make_async_copy(rows_hbm.at[320:], rows_ref.at[320:], fetch_sems.at[4]))
    fetches.append(pltpu.make_async_copy(down_hbm, down_ref, fetch_sems.at[5]))
    for fetch in fetches:
        fetch.start()
    fetches[0].wait()
    copies = []
    for part in range(2):
        rows = slice(part * 320, (part + 1) * 320)
        if part == 0:
            for i in range(3):
                lanes = slice(widths[i], widths[i + 1])
                fetches[1 + i].wait()
                product_ref[:, lanes] = jnp.dot(
                    rows_ref[rows, :], gate_up_ref[:, lanes], preferred_element_type=jnp.float32
                )
            gate_up = product_ref[...]
            fetches[4].wait()
            fetches[5].wait()
        else:
            gate_up = jnp.dot(
                rows_ref[rows, :], gate_up_ref[...], preferred_element_type=jnp.float32
            )
        hidden = (jax.nn.silu(gate_up[:, :units]) * gate_up[:, units:]).astype(jnp.bfloat16)
        for f in range(8):
            result = jnp.dot(
                hidden, down_ref[:, f * 256 : (f + 1) * 256], preferred_element_type=jnp.float32
            )
            for r in range(8):
                out_ref[part * 8 + r, f] = result[r * 40 : (r + 1) * 40].astype(jnp.bfloat16)
            there = (pl.ds(part * 8, 8), f)
            copies.append(
                pltpu.make_async_copy(out_ref.at[there], out_hbm.at[there], sems.at[part * 8 + f])
            )
            copies[-1].start()
    for copy in copies:
        copy.wait()


def expert(rows, gate_up, down):
    return pl.pallas_call(
        expert_kernel,
        in_specs=in_hbm(3),
        out_specs=in_hbm(1)[0],
        out_shape=jax.ShapeDtypeStruct((16, 8, 40, 256), jnp.bfloat16),
        scratch_shapes=[
            pltpu.VMEM(rows.shape, jnp.bfloat16),
            pltpu.VMEM(gate_up.shape, jnp.bfloat16),
            pltpu.VMEM(down.shape, jnp.bfloat16),
            pltpu.VMEM((16, 8, 40, 256), jnp.bfloat16),
            pltpu.VMEM((320, gate_up.shape[1]), jnp.float32),
            pltpu.SemaphoreType.DMA((6,)),
            pltpu.SemaphoreType.DMA((16,)),
        ],
        compiler_params=pltpu.CompilerParams(vmem_limit_bytes=60 << 20),
        name="expert",
    )(rows, gate_up, down)


def place_rows_kernel(dest_ref, *refs):
    out_ref = refs[-1]
    total = jnp.zeros(out_ref.shape, jnp.float32)
    at = 0
    for ref in refs[:-1]:
        height = ref.shape[0]
        dest = dest_ref[:, at : at + height]
        rows = lax.broadcasted_iota(jnp.int32, (out_ref.shape[0], height), 0)
        mover = jnp.where(rows == dest, 1.0, 0.0).astype(jnp.bfloat16)
        total += jnp.dot(mover, ref[...], preferred_element_type=jnp.float32)
        at += height
    out_ref[...] = total.astype(out_ref.dtype)


def place_rows(dest, sources):
    return pl.pallas_call(
        place_rows_kernel,
        out_shape=jax.ShapeDtypeStruct((256, sources[0].shape[1]), sources[0].dtype),
        compiler_params=pltpu.CompilerParams(vmem_limit_bytes=8 << 20),
        name="place_rows",
    )(dest, *sources)


def on_device(
    tokens,
    attn_gain,
    mlp_gain,
    trainer_qkv,
    trainer_out,
    router,
    shared_gate,
    shared_up,
    shared_down,
    expert_gate_up,
    expert_down,
    lengths,
    order,
    routes,
):
    tok_rows = tokens.shape[0]
    row_count, col_count = 16, 8
    zh_index = lax.axis_index("zh")
    y_index = lax.axis_index("y")
    k_index = lax.axis_index("k")
    row_index = lax.axis_index(ROW)
    col_index = lax.axis_index(COL)
    first = row_index * tok_rows
    local = jnp.arange(tok_rows, dtype=jnp.int32)

    seg_query, within_query, _ = prompt_tables(lengths, order, first + local)
    cosine, sine_part = rotary_tables(within_query, HEAD_DIM)
    packed = jnp.sum(
        jnp.where(order[:, None] == jnp.arange(8, dtype=jnp.int32)[None, :], lengths[None, :], 0), axis=1
    )
    start = jnp.cumsum(packed) - packed

    heads = trainer_qkv.astype(jnp.bfloat16).reshape(16, 24, HEAD_DIM).transpose(1, 0, 2)
    groups = jnp.stack(
        [jnp.stack([heads[2 * g], heads[2 * g + 1], heads[16 + g // 2], heads[20 + g // 2]]) for g in range(8)]
    ).reshape(8, 64, HEAD_DIM)
    token_parts = tokens.reshape(tok_rows, 2, HEAD_DIM).transpose(1, 0, 2).reshape(1, 512, HEAD_DIM)
    out_parts = (
        trainer_out.astype(jnp.bfloat16).T.reshape(16, 8, 2, HEAD_DIM).transpose(1, 2, 0, 3)
    ).reshape(8, 32, HEAD_DIM)
    came = lax.all_to_all(
        jnp.concatenate(
            [groups, jnp.broadcast_to(token_parts, (8, 512, HEAD_DIM)), out_parts], axis=1
        ),
        COL, 0, 0, tiled=True,
    )
    qkv_heads = came[:, :64].reshape(8, 4, 16, HEAD_DIM).transpose(1, 0, 2, 3).reshape(4, 128, HEAD_DIM)
    out_rows = came[:, 576:].reshape(8, 2, 16, HEAD_DIM).transpose(1, 3, 0, 2).reshape(256, 128)

    block = jnp.concatenate([qkv_heads.reshape(512, HEAD_DIM), out_rows], axis=0)
    mine = lax.all_to_all(
        jnp.broadcast_to(block[None], (8, 768, HEAD_DIM)), ("zh", "y"), 0, 0, tiled=True
    )
    other = core_swap(mine)

    queries, kv_rows = projection(
        came, mine, other, attn_gain.reshape(16, HEAD_DIM), cosine, sine_part
    )
    cache_out = jnp.where(col_index % 2 == 0, kv_rows[:, :HEAD_DIM], kv_rows[:, HEAD_DIM:])

    head_sent = lax.ppermute(kv_rows[128:], ROW, [(7, 15)])
    block = jnp.concatenate([kv_rows, head_sent], axis=0)
    kv_mine = lax.all_to_all(
        jnp.broadcast_to(block[None], (4, 384, 256)), "y", 0, 0, tiled=True
    )
    kv_other = core_swap(kv_mine)
    terms, qkv_block, out_block = attention(queries, kv_mine, kv_other, start, mine, other)
    got = lax.all_to_all(terms, COL, 0, 0, tiled=True)
    attn_part = jnp.sum(got.astype(jnp.float32), axis=0)
    resid = (tokens.astype(jnp.float32) + attn_part).astype(jnp.bfloat16)
    full_resid = col_gather(resid)

    n_experts = row_count * col_count // 2
    capacity = 40
    expert_ids = jnp.arange(n_experts, dtype=jnp.int32)
    member = jnp.any(routes[:, :, None] == expert_ids[None, None, :], axis=1)
    slot_of = jnp.where(member, jnp.cumsum(member.astype(jnp.int32), axis=0) - 1, -1)
    by_quarter = slot_of.reshape(tok_rows, row_count, col_count // 2)
    quarter = col_index // 2
    straight = lax.dynamic_index_in_dim(by_quarter, quarter, 2, keepdims=False)
    crossed = lax.dynamic_index_in_dim(by_quarter, quarter ^ 2, 2, keepdims=False)
    same_half = (jnp.arange(row_count) // 8 == zh_index)[None, :]
    slots = jnp.where(same_half, straight, crossed).T
    outgoing = dispatch(full_resid, mlp_gain[None, :], slots)
    arrived = lax.all_to_all(
        outgoing, ROW + COL, 0, 0, axis_index_groups=DIAGONALS, tiled=True
    )

    shared_part, logits = shared(
        full_resid, mlp_gain[None, :], router.T, shared_gate.T, shared_up.T, shared_down
    )
    router_probs = jax.nn.softmax(logits, axis=-1)
    picked_probs = jnp.where(member, router_probs, 0.0)
    route_weight = (
        picked_probs / jnp.sum(picked_probs, axis=-1, keepdims=True)
    ).astype(jnp.bfloat16)
    twice = jnp.repeat(slot_of, 2, axis=1)[:, :, None]
    combiner = jnp.where(
        twice == jnp.arange(capacity, dtype=jnp.int32),
        jnp.repeat(route_weight, 2, axis=1)[:, :, None],
        jnp.bfloat16(0),
    ).reshape(tok_rows, 2 * n_experts * capacity)
    pieces = []
    for step in range(col_count):
        piece = shared_part[step]
        if step:
            piece = lax.ppermute(piece, COL, [(i, i ^ step) for i in range(col_count)])
        pieces.append(piece)
    arrived, combiner, pieces, cache_out = lax.optimization_barrier(
        (arrived, combiner, pieces, cache_out)
    )
    shared_sum = sum(piece.astype(jnp.float32) for piece in pieces)

    result = expert(
        arrived.reshape(row_count * capacity, D), expert_gate_up[0], expert_down[0]
    )
    came_back = lax.all_to_all(
        result.reshape(2 * n_experts, capacity, 256), ROW + COL, 0, 0, tiled=True
    )
    routed_part = jnp.dot(
        combiner,
        came_back.reshape(2 * n_experts * capacity, 256),
        preferred_element_type=jnp.float32,
    )
    layer_out = (
        resid.astype(jnp.float32) + shared_sum + routed_part
    ).astype(jnp.bfloat16)

    received = []
    for step in range(4):
        pairs = [(s, 4 + (s + step) % 4) for s in range(4)]
        if step == 0:
            pairs += [(4 + s, s) for s in range(4)]
        received.append(lax.ppermute(layer_out, ("zh", "y"), pairs))
    late = lax.ppermute(
        layer_out[128:], ROW, [(7 + i, i) for i in range(0, 8, 2)] + [(15, 8)]
    )
    swapped = [core_swap(rows) for rows in received]
    span = jnp.arange(1024, dtype=jnp.int32)
    step_of = span // 256
    from_row = jnp.where(
        zh_index == 1,
        ((y_index - step_of) % 4) * 2,
        jnp.where(step_of == 0, 8 + y_index * 2, jnp.int32(1 << 12)),
    )
    late_from = jnp.where(
        k_index == 1, 1 << 12, jnp.where(zh_index == 0, row_index + 7, jnp.where(row_index == 8, 15, 1 << 12))
    )
    source_pos = jnp.concatenate(
        [
            (from_row + k_index) * 256 + span % 256,
            (from_row + 1 - k_index) * 256 + span % 256,
            late_from * 256 + 128 + jnp.arange(128, dtype=jnp.int32),
        ]
    )
    _, _, dest = prompt_tables(lengths, order, source_pos)
    dest = jnp.where(source_pos < row_count * tok_rows, dest, -1)
    hidden_states = place_rows((dest - first)[None, :], received + swapped + [late])
    return (hidden_states, cache_out, qkv_block, out_block)


def solution(mesh):
    fine = Mesh(mesh.devices.reshape(2, 4, 2, 2, 4), ROW + COL)
    in_specs = (
        P(ROW, COL),
        P(),
        P(),
        P(ROW + COL, None),
        P(None, ROW + COL),
        P(),
        P(None, COL),
        P(None, COL),
        P(COL, None),
        P(ROW + COL, None, None),
        P(ROW + COL, None, None),
        P(),
        P(),
        P(ROW, None),
    )
    out_specs = (P(ROW, COL), P(ROW, COL), P(ROW, COL), P(COL, ROW))
    return jax.shard_map(
        on_device, mesh=fine, in_specs=in_specs, out_specs=out_specs, check_vma=False
    )
```
